32 devices in a mesh: view: 8 (over y, x, core), row: 4 (over z).
Axes of the slice: x: 2, y: 2, z: 4, core: 2. Of those that a mesh axis runs over, the one named last changes fastest.
Arguments:
- queries: bfloat16 [8, 16, 64, 2048], P('view', 'row'), may hold values from -60 to 60
- target_keys: bfloat16 [8, 16, 64, 2048], P('view', 'row'), may hold values from -6 to 6
- target_values: bfloat16 [8, 16, 64, 2048], P('view', 'row'), may hold values from -6 to 6
- cond_keys: bfloat16 [512, 2048], P(('view', 'row')), may hold values from -21 to 21
- cond_values: bfloat16 [512, 2048], P(('view', 'row')), may hold values from -6 to 6
Outputs:
- attended: bfloat16 [8, 16, 64, 2048], P('view', 'row')
The draws below stay inside these ranges and needn't reach their ends.
All inputs are finite; a program needn't handle non-finite values.
Results may differ from the reference program's by a relative error of at most 0.0089.
Values may be sent and summed in bfloat16 or wider, within the bound.
No kernel may reach another device: no remote copies, remote signals or barrier semaphores. Data moves between devices by JAX's collectives and lax.ppermute only.
A program may use at most 64 MiB of HBM per device.

```python
import jax
import jax.numpy as jnp
from jax import lax

HEADS = 16
HD = 128
RADIUS = 8
COLS = 64
VIEWS = 8
ROWS = 16
CTOK = 512


def draw_queries(key, part):
    shape = (VIEWS, ROWS, COLS, HEADS, HD)
    drawn = 2.0 * jax.random.truncated_normal(jax.random.fold_in(key, 11), -3.0, 3.0, shape, jnp.float32)
    return drawn.reshape(VIEWS, ROWS, COLS, HEADS * HD).astype(jnp.bfloat16)


def draw_cond_keys(key, part):
    shape = (CTOK, HEADS, HD)
    drawn = jax.random.truncated_normal(jax.random.fold_in(key, 21), -6.0, 6.0, shape, jnp.float32)
    return drawn.reshape(CTOK, HEADS * HD).astype(jnp.bfloat16)


def block_levels(stream_key, shape, split, least, largest):
    def one(position, shards_of):
        draws = jax.random.uniform(jax.random.fold_in(jax.random.fold_in(stream_key, 6), position), (shards_of,), jnp.float32, least / len(split), largest / len(split))
        return jnp.repeat(jnp.exp(draws), shape[position] // shards_of).reshape((-1,) + (1,) * (len(shape) - position - 1))

    gain = one(*split[0])
    for cut in split[1:]:
        gain = gain * one(*cut)
    return gain


def bell_draw(rng, shape, spread, bound, pieces=(), held_as=jnp.bfloat16):
    values = spread * jax.random.normal(rng, shape, jnp.float32)
    if pieces:
        values = values * block_levels(rng, shape, pieces, -0.22, 0.18)
    return jnp.clip(values, -bound, bound).astype(held_as)


def setup_inputs(seed: int = 0) -> dict:
    keys = jax.random.split(jax.random.key(seed), 6)
    queries = draw_queries(jax.random.fold_in(keys[5], 71), 0)
    target_keys = bell_draw(keys[1], (VIEWS, ROWS, COLS, HEADS * HD), 1.0, 6.0, ((0, 8), (1, 4)))
    target_values = bell_draw(keys[2], (VIEWS, ROWS, COLS, HEADS * HD), 1.0, 6.0, ((0, 8), (1, 4)))
    cond_keys = draw_cond_keys(jax.random.fold_in(keys[5], 71), 0)
    cond_values = bell_draw(keys[4], (CTOK, HEADS * HD), 1.0, 6.0, ((0, 32),))
    return dict(queries=queries, target_keys=target_keys, target_values=target_values, cond_keys=cond_keys, cond_values=cond_values)


BASE = 10000.0
NEG_FILL = -1.0e30


def group_layout(head_dim):
    view_width = head_dim // 4
    row_width = 3 * head_dim // 8
    return ((0, view_width), (view_width, row_width), (view_width + row_width, head_dim - view_width - row_width))


def rotary(features, coords):
    outputs = []
    for group_index, (offset, group_width) in enumerate(group_layout(features.shape[-1])):
        half_width = group_width // 2
        lower_part = features[..., offset:offset + half_width]
        upper_part = features[..., offset + half_width:offset + group_width]
        frequency = jnp.power(BASE, -jnp.arange(half_width, dtype=jnp.float32) / half_width)
        angles = coords[..., group_index][..., None, None] * frequency
        cosine = jnp.cos(angles)
        sine = jnp.sin(angles)
        outputs.append(lower_part * cosine - upper_part * sine)
        outputs.append(upper_part * cosine + lower_part * sine)
    return jnp.concatenate(outputs, axis=-1)


def widen(array):
    return lax.optimization_barrier(array).astype(jnp.float32)


def reference(queries, target_keys, target_values, cond_keys, cond_values):
    scale = HD ** -0.5
    span = 2 * RADIUS + 1
    cond_index = jnp.arange(CTOK, dtype=jnp.int32)
    cond_coords = jnp.stack([jnp.zeros((CTOK,), jnp.float32), (cond_index // COLS).astype(jnp.float32), (cond_index % COLS).astype(jnp.float32)], axis=-1)
    cond_rot = widen(rotary(cond_keys.astype(jnp.float32).reshape(CTOK, HEADS, HD), cond_coords).astype(jnp.bfloat16))
    cond_vals = cond_values.astype(jnp.float32).reshape(CTOK, HEADS, HD)
    grid_rows = jnp.broadcast_to(jnp.arange(ROWS, dtype=jnp.int32)[:, None], (ROWS, COLS)).astype(jnp.float32)
    grid_cols = jnp.broadcast_to(jnp.arange(COLS, dtype=jnp.int32)[None, :], (ROWS, COLS)).astype(jnp.float32)
    col_ids = jnp.arange(COLS, dtype=jnp.int32)
    col_ok = jnp.abs(col_ids[:, None] - col_ids[None, :]) <= RADIUS

    def one_view(operands):
        view_queries, view_keys, view_values, view_id = operands
        view_coord = jnp.ones((ROWS, COLS), jnp.float32) * (view_id + 1).astype(jnp.float32)
        coords = jnp.stack([view_coord, grid_rows, grid_cols], axis=-1)
        q_rot = widen(rotary(view_queries.astype(jnp.float32).reshape(ROWS, COLS, HEADS, HD), coords).astype(jnp.bfloat16))
        k_rot = widen(rotary(view_keys.astype(jnp.float32).reshape(ROWS, COLS, HEADS, HD), coords).astype(jnp.bfloat16))
        padding = ((RADIUS, RADIUS), (0, 0), (0, 0), (0, 0))
        keys_pad = jnp.pad(k_rot, padding)
        values_pad = jnp.pad(view_values.astype(jnp.float32).reshape(ROWS, COLS, HEADS, HD), padding)

        def one_row(row_id):
            row_queries = lax.dynamic_index_in_dim(q_rot, row_id, 0, keepdims=False)
            band_keys = lax.dynamic_slice_in_dim(keys_pad, row_id, span, 0).reshape(span * COLS, HEADS, HD)
            band_values = lax.dynamic_slice_in_dim(values_pad, row_id, span, 0).reshape(span * COLS, HEADS, HD)
            band_rows = row_id + jnp.arange(span, dtype=jnp.int32) - RADIUS
            row_ok = (band_rows >= 0) & (band_rows < ROWS)
            allowed = (row_ok[None, :, None] & col_ok[:, None, :]).reshape(COLS, span * COLS)
            win_scores = jnp.einsum("chd,khd->hck", row_queries, band_keys) * scale
            win_scores = jnp.where(allowed[None], win_scores, NEG_FILL)
            cond_scores = jnp.einsum("chd,nhd->hcn", row_queries, cond_rot) * scale
            row_max = jnp.maximum(jnp.max(win_scores, axis=-1), jnp.max(cond_scores, axis=-1))
            win_weights = jnp.exp(win_scores - row_max[..., None])
            cond_weights = jnp.exp(cond_scores - row_max[..., None])
            denominator = jnp.sum(win_weights, axis=-1) + jnp.sum(cond_weights, axis=-1)
            summed = jnp.einsum("hck,khd->hcd", widen(win_weights.astype(jnp.bfloat16)), band_values)
            summed = summed + jnp.einsum("hcn,nhd->hcd", widen(cond_weights.astype(jnp.bfloat16)), cond_vals)
            result = summed / denominator[..., None]
            return result.transpose(1, 0, 2).reshape(COLS, HEADS * HD).astype(jnp.bfloat16)

        return lax.map(one_row, jnp.arange(ROWS, dtype=jnp.int32))

    return lax.map(one_view, (queries, target_keys, target_values, jnp.arange(VIEWS, dtype=jnp.int32)))
```

```python
import functools

import jax
import jax.numpy as jnp
import numpy as np
from jax import lax
from jax.experimental import pallas as pl
from jax.experimental.pallas import tpu as pltpu
from jax.sharding import PartitionSpec as P

HD = 128
RADIUS = 8
BASE = 10000.0
NEG = -1e30
EXP_SCALE = HD ** (-0.5) * float(np.log2(np.e))


def group_layout(head_dim):
    view_width = head_dim // 4
    row_width = 3 * head_dim // 8
    return (
        (0, view_width),
        (view_width, row_width),
        (view_width + row_width, head_dim - view_width - row_width),
    )


def axis_table(group_index, count):
    offset, width = group_layout(HD)[group_index]
    half = width // 2
    frequency = BASE ** (-np.arange(half, dtype=np.float64) / half)
    angles = np.arange(count, dtype=np.float64)[:, None] * frequency
    cosine = np.zeros((count, HD), np.float32)
    sine = np.zeros((count, HD), np.float32)
    for start in (offset, offset + half):
        cosine[:, start : start + half] = np.cos(angles)
        sine[:, start : start + half] = np.sin(angles)
    return np.stack([cosine, sine])


def partner_matrix():
    m = np.zeros((HD, HD), np.float32)
    for offset, width in group_layout(HD):
        half = width // 2
        for i in range(half):
            m[offset + half + i, offset + i] = -1.0
            m[offset + i, offset + half + i] = 1.0
    return m


def window_bias(rows, cols, row_shift):
    row = np.arange(rows * cols) // cols
    col = np.arange(rows * cols) % cols
    row_ok = np.abs(row[None, :] + row_shift - row[:, None]) <= RADIUS
    col_ok = np.abs(col[None, :] - col[:, None]) <= RADIUS
    return np.where(row_ok & col_ok, 0.0, NEG).astype(np.float32)


def rotated(x, partners, cosine, sine):
    swapped = jnp.dot(x, partners, preferred_element_type=jnp.float32)
    return (x.astype(jnp.float32) * cosine + swapped * sine).astype(jnp.bfloat16)


def cond_kernel(keys_ref, values_ref, table_ref, partners_ref, out_ref):
    for start in range(0, keys_ref.shape[1], HD):
        span = pl.ds(start, HD)
        out_ref[0, :, span] = rotated(
            keys_ref[:, span], partners_ref[...], table_ref[0], table_ref[1]
        )
    out_ref[1] = values_ref[...]


def rotate_kernel(q_ref, k_ref, table_ref, partners_ref, qo_ref, ko_ref):
    for start in range(0, q_ref.shape[1], HD):
        span = pl.ds(start, HD)
        for source, target in ((k_ref, ko_ref), (q_ref, qo_ref)):
            target[:, span] = rotated(
                source[:, span], partners_ref[...], table_ref[0], table_ref[1]
            )


def attend_kernel(blocks, first, last, group, *refs):
    refs = list(refs)
    valid_ref = refs.pop(0)
    q_ref = refs.pop(0)
    if not first:
        acc_in, ml_in = refs.pop(0), refs.pop(0)
    sources = []
    for kind, bias, _ in blocks:
        if kind == "cond":
            kv = refs.pop(0)
            sources.append((kv.at[0], kv.at[1], None))
        else:
            sources.append((refs.pop(0), refs.pop(0), None))
    biases = []
    for _, bias, _ in blocks:
        biases.append(refs.pop(0) if bias is not None else None)
    if last:
        out_ref = refs.pop(0)
    else:
        acc_out, ml_out = refs.pop(0), refs.pop(0)
    acc_ref, m_ref, l_ref = refs
    tokens = q_ref.shape[0]
    lanes = lax.broadcasted_iota(jnp.int32, (tokens, HD), 1)
    ml = jnp.zeros((tokens, HD), jnp.float32)
    for head in range(group):
        span = pl.ds(head * HD, HD)
        q = q_ref[:, span]
        have = not first
        if have:
            acc_ref[...] = acc_in[:, span]
            m_ref[...] = ml_in[0, :, head : head + 1]
            l_ref[...] = ml_in[0, :, group + head : group + head + 1]
        for (kind, bias, flag), (k_ref, v_ref, _), bias_ref in zip(blocks, sources, biases):

            def step(have=have, k_ref=k_ref, v_ref=v_ref, bias_ref=bias_ref):
                s = lax.dot_general(
                    q, k_ref[:, span], (((1,), (1,)), ((), ())),
                    preferred_element_type=jnp.float32,
                )
                if bias_ref is not None:
                    s = s + bias_ref[...]
                top = jnp.max(s, axis=1, keepdims=True)
                if have:
                    m_old = m_ref[...]
                    top = jnp.maximum(top, m_old)
                p = jnp.exp2((s - top) * EXP_SCALE)
                total = jnp.sum(p, axis=1, keepdims=True)
                pv = jnp.dot(
                    p.astype(jnp.bfloat16), v_ref[:, span], preferred_element_type=jnp.float32
                )
                if have:
                    alpha = jnp.exp2((m_old - top) * EXP_SCALE)
                    total = total + l_ref[...] * alpha
                    pv = pv + acc_ref[...] * alpha
                m_ref[...] = top
                l_ref[...] = total
                acc_ref[...] = pv

            if flag is None:
                step()
            else:
                pl.when(valid_ref[flag] != 0)(step)
            have = True
        if last:
            out_ref[:, span] = (acc_ref[...] / l_ref[...]).astype(out_ref.dtype)
        else:
            acc_out[:, span] = acc_ref[...]
            ml = jnp.where(lanes == head, m_ref[...], ml)
            ml = jnp.where(lanes == group + head, l_ref[...], ml)
    if not last:
        ml_out[0] = ml


def attend(valid, q, state, sources, blocks, last, group):
    tokens, width = q.shape
    steps = width // HD // group
    lane_block = pl.BlockSpec((tokens, group * HD), lambda g, _: (0, g))
    ml_block = pl.BlockSpec((1, tokens, HD), lambda g, _: (g, 0, 0))
    operands = [q]
    specs = [lane_block]
    if state is not None:
        operands += list(state)
        specs += [lane_block, ml_block]
    flops = 0
    for (kind, _, _), source in zip(blocks, sources):
        operands += list(source)
        for array in source:
            if array.ndim == 3:
                specs.append(
                    pl.BlockSpec((2, array.shape[1], group * HD), lambda g, _: (0, 0, g))
                )
                count = array.shape[1]
            else:
                specs.append(
                    pl.BlockSpec((array.shape[0], group * HD), lambda g, _: (0, g))
                )
                count = array.shape[0]
        flops += 4 * tokens * count * width
    for _, bias, _ in blocks:
        if bias is not None:
            operands.append(jnp.asarray(bias))
            specs.append(pl.BlockSpec(bias.shape, lambda g, _: (0, 0)))
    if last:
        out_shape = jax.ShapeDtypeStruct((tokens, width), jnp.bfloat16)
        out_specs = lane_block
    else:
        out_shape = (
            jax.ShapeDtypeStruct((tokens, width), jnp.float32),
            jax.ShapeDtypeStruct((steps, tokens, HD), jnp.float32),
        )
        out_specs = (lane_block, ml_block)
    moved = sum(a.size * a.dtype.itemsize for a in operands) + tokens * width * 4
    return pl.pallas_call(
        functools.partial(attend_kernel, blocks, state is None, last, group),
        out_shape=out_shape,
        grid_spec=pltpu.PrefetchScalarGridSpec(
            num_scalar_prefetch=1,
            grid=(steps,),
            in_specs=specs,
            out_specs=out_specs,
            scratch_shapes=[
                pltpu.VMEM((tokens, HD), jnp.float32),
                pltpu.VMEM((tokens, 1), jnp.float32),
                pltpu.VMEM((tokens, 1), jnp.float32),
            ],
        ),
        cost_estimate=pl.CostEstimate(
            flops=flops, bytes_accessed=moved, transcendentals=flops // (4 * HD)
        ),
    )(valid, *operands)


def passed_along(x, axis, by):
    length = lax.axis_size(axis)
    pairs = [(i, i + by) for i in range(length) if 0 <= i + by < length]
    return lax.ppermute(x, axis, pairs)


def gathered(piece, axes):
    held = (piece,)
    for axis in axes:
        distance = lax.axis_size(axis) // 2
        while distance:
            whole = jnp.concatenate(held, axis=1) if len(held) > 1 else held[0]
            pairs = [(i, i ^ distance) for i in range(lax.axis_size(axis))]
            held = (whole, lax.ppermute(whole, axis, pairs))
            distance //= 2
    return held


def local(queries, target_keys, target_values, cond_keys, cond_values):
    view_dev, rows_dev, cols, width = queries.shape
    heads = width // HD
    row_count = lax.axis_size("row")
    view_count = lax.axis_size("view")
    tokens = rows_dev * cols
    row_index = lax.axis_index("row")
    view_index = lax.axis_index("view")
    ctok_dev = cond_keys.shape[0]
    ctok = ctok_dev * view_count * row_count
    group = 2 if heads % 2 == 0 else 1

    partners = jnp.asarray(partner_matrix(), jnp.bfloat16)
    view_table = axis_table(0, view_count * view_dev + 1)
    row_table = axis_table(1, max(row_count * rows_dev, -(-ctok // cols)))
    col_table = axis_table(2, cols)

    cond_ids = np.arange(ctok)
    cond_table = view_table[:, :1] + row_table[:, cond_ids // cols] + col_table[:, cond_ids % cols]
    cond_base = (view_index * row_count + row_index) * ctok_dev
    cond_slice = lax.dynamic_slice_in_dim(jnp.asarray(cond_table), cond_base, ctok_dev, axis=1)
    piece = pl.pallas_call(
        cond_kernel, out_shape=jax.ShapeDtypeStruct((2, ctok_dev, width), jnp.bfloat16)
    )(cond_keys, cond_values, cond_slice, partners)
    cond_held = gathered(piece, ("row", "view"))

    view_dev_ids = view_index * view_dev + 1
    tables = lax.dynamic_slice_in_dim(jnp.asarray(view_table), view_dev_ids, view_dev, axis=1)
    rows_here = lax.dynamic_slice_in_dim(
        jnp.asarray(row_table), row_index * rows_dev, rows_dev, axis=1
    )
    place = (rows_here[:, :, None] + jnp.asarray(col_table)[:, None]).reshape(2, tokens, HD)

    reach = -(-RADIUS // rows_dev)
    near = [d for d in range(1, reach)]
    flags = []
    for d in range(1, reach + 1):
        flags += [row_index - d >= 0, row_index + d < row_count]
    valid = jnp.stack(flags).astype(jnp.int32)

    outputs = []
    for v in range(view_dev):
        values = target_values[v].reshape(tokens, width)
        table = tables[:, v : v + 1] + place
        lane_block = pl.BlockSpec((tokens, 4 * HD), lambda g: (0, g))
        q_rot, k_rot = pl.pallas_call(
            rotate_kernel,
            out_shape=(jax.ShapeDtypeStruct((tokens, width), jnp.bfloat16),) * 2,
            grid=(heads // 4,),
            in_specs=[
                lane_block,
                lane_block,
                pl.BlockSpec((2, tokens, HD), lambda g: (0, 0, 0)),
                pl.BlockSpec((HD, HD), lambda g: (0, 0)),
            ],
            out_specs=(lane_block, lane_block),
            cost_estimate=pl.CostEstimate(
                flops=4 * tokens * width * HD,
                bytes_accessed=8 * tokens * width,
                transcendentals=0,
            ),
        )(
            queries[v].reshape(tokens, width),
            target_keys[v].reshape(tokens, width),
            table,
            partners,
        )
        from_above, from_below = [values], [values]
        above, below = [], []
        for d in range(reach):
            from_above.append(passed_along(from_above[-1], "row", 1))
            from_below.append(passed_along(from_below[-1], "row", -1))
        keys_above, keys_below = k_rot, k_rot
        for d in range(1, reach + 1):
            keys_above = passed_along(keys_above, "row", 1)
            keys_below = passed_along(keys_below, "row", -1)
            above.append((keys_above, from_above[d]))
            below.append((keys_below, from_below[d]))

        def block_of(d, sign):
            return ("window", window_bias(rows_dev, cols, sign * d * rows_dev),
                    2 * (d - 1) + (sign > 0))

        state = attend(
            valid, q_rot, None,
            [(k_rot, values)] + [s for d in near for s in (above[d - 1], below[d - 1])],
            [("window", window_bias(rows_dev, cols, 0), None)]
            + [b for d in near for b in (block_of(d, -1), block_of(d, 1))],
            False, group,
        )
        state = attend(
            valid, q_rot, state, [(c,) for c in cond_held],
            [("cond", None, None)] * len(cond_held), False, group,
        )
        out = attend(
            valid, q_rot, state, [above[reach - 1], below[reach - 1]],
            [block_of(reach, -1), block_of(reach, 1)], True, group,
        )
        outputs.append(out.reshape(rows_dev, cols, width))
    return jnp.stack(outputs) if view_dev > 1 else outputs[0][None]


def solution(mesh):
    return jax.shard_map(
        local,
        mesh=mesh,
        in_specs=(
            P("view", "row", None, None),
            P("view", "row", None, None),
            P("view", "row", None, None),
            P(("view", "row"), None),
            P(("view", "row"), None),
        ),
        out_specs=P("view", "row", None, None),
        check_vma=False,
    )
```

```python
import functools

import jax
import jax.numpy as jnp
import numpy as np
from jax import lax
from jax.experimental import pallas as pl
from jax.experimental.pallas import tpu as pltpu
from jax.sharding import PartitionSpec as P


HD = 128
RADIUS = 8
BASE = 10000.0
NEG = -1e30
EXP_SCALE = HD ** (-0.5) * float(np.log2(np.e))


def group_layout(head_dim):
    view_width = head_dim // 4
    row_width = 3 * head_dim // 8
    return (
        (0, view_width),
        (view_width, row_width),
        (view_width + row_width, head_dim - view_width - row_width),
    )


def axis_table(group_index, count):
    offset, width = group_layout(HD)[group_index]
    half = width // 2
    frequency = BASE ** (-np.arange(half, dtype=np.float64) / half)
    angles = np.arange(count, dtype=np.float64)[:, None] * frequency
    cosine = np.zeros((count, HD), np.float32)
    sine = np.zeros((count, HD), np.float32)
    for start in (offset, offset + half):
        cosine[:, start : start + half] = np.cos(angles)
        sine[:, start : start + half] = np.sin(angles)
    return np.stack([cosine, sine])


def partner_matrix():
    m = np.zeros((HD, HD), np.float32)
    for offset, width in group_layout(HD):
        half = width // 2
        for i in range(half):
            m[offset + half + i, offset + i] = -1.0
            m[offset + i, offset + half + i] = 1.0
    return m


def window_bias(rows, cols, row_shift):
    row = np.arange(rows * cols) // cols
    col = np.arange(rows * cols) % cols
    row_ok = np.abs(row[None, :] + row_shift - row[:, None]) <= RADIUS
    col_ok = np.abs(col[None, :] - col[:, None]) <= RADIUS
    return np.where(row_ok & col_ok, 0.0, NEG).astype(np.float32).T


def rotated(x, partners, cosine, sine):
    swapped = jnp.dot(x, partners, preferred_element_type=jnp.float32)
    return (x.astype(jnp.float32) * cosine + swapped * sine).astype(jnp.bfloat16)


def cond_kernel(keys_ref, values_ref, table_ref, partners_ref, out_ref):
    for start in range(0, keys_ref.shape[1], HD):
        span = pl.ds(start, HD)
        out_ref[0, :, span] = rotated(
            keys_ref[:, span], partners_ref[...], table_ref[0], table_ref[1]
        )
    out_ref[1] = values_ref[...]


def rotate_kernel(q_ref, k_ref, table_ref, partners_ref, qo_ref, ko_ref):
    for start in range(0, q_ref.shape[1], HD):
        span = pl.ds(start, HD)
        for source, target in ((k_ref, ko_ref), (q_ref, qo_ref)):
            target[:, span] = rotated(
                source[:, span], partners_ref[...], table_ref[0], table_ref[1]
            )


def attend_kernel(stages, first, last, group, *refs):
    refs = list(refs)
    valid_ref, q_ref = refs.pop(0), refs.pop(0)
    if not first:
        acc_in, ml_in = refs.pop(0), refs.pop(0)
    pulled = [[(refs.pop(0), refs.pop(0)) for _ in blocks] for _, blocks in stages]
    biases = [[refs.pop(0) if bias is not None else None for bias in blocks] for _, blocks in stages]
    if last:
        out_ref, acc_ref, ml_ref = refs
    else:
        acc_ref, ml_ref = refs
        ml_ref = ml_ref.at[0]
    if not first:
        acc_ref[...] = acc_in[...]
        ml_ref[...] = ml_in[0]

    def stage(sources, masks, have):
        for head in range(group):
            span = pl.ds(head * HD, HD)
            m_row, l_row = pl.ds(head, 1), pl.ds(group + head, 1)
            q = q_ref[:, span]
            scores = []
            for (k_ref, _), bias_ref in zip(sources, masks):
                s = lax.dot_general(
                    k_ref[:, span], q, (((1,), (1,)), ((), ())),
                    preferred_element_type=jnp.float32,
                )
                scores.append(s if bias_ref is None else s + bias_ref[...])
            top = functools.reduce(
                jnp.maximum, [jnp.max(s, axis=0, keepdims=True) for s in scores]
            )
            if have:
                m_old = ml_ref[m_row, :]
                top = jnp.maximum(top, m_old)
                alpha = jnp.exp2((m_old - top) * EXP_SCALE)
                total = ml_ref[l_row, :] * alpha
                summed = acc_ref[span, :] * alpha
            else:
                total = summed = 0.0
            for s, (_, v_ref) in zip(scores, sources):
                p = jnp.exp2((s - top) * EXP_SCALE)
                total = total + jnp.sum(p, axis=0, keepdims=True)
                summed = summed + lax.dot_general(
                    v_ref[:, span], p.astype(jnp.bfloat16), (((0,), (0,)), ((), ())),
                    preferred_element_type=jnp.float32,
                )
            ml_ref[m_row, :] = top
            ml_ref[l_row, :] = total
            acc_ref[span, :] = summed

    have = not first
    for (flag, _), sources, masks in zip(stages, pulled, biases):
        step = functools.partial(stage, sources, masks, have)
        if flag is None:
            step()
        else:
            pl.when(valid_ref[flag] != 0)(step)
        have = True
    if last:
        for head in range(group):
            span = pl.ds(head * HD, HD)
            scaled = acc_ref[span, :] * (1.0 / ml_ref[pl.ds(group + head, 1), :])
            out_ref[:, span] = scaled.astype(out_ref.dtype).T


def attend(valid, q, state, sources, stages, last, group):
    tokens, width = q.shape
    steps = width // HD // group
    lane_block = pl.BlockSpec((tokens, group * HD), lambda g, _: (0, g))
    acc_block = pl.BlockSpec((group * HD, tokens), lambda g, _: (g, 0))
    ml_block = pl.BlockSpec((1, 2 * group, tokens), lambda g, _: (g, 0, 0))
    operands = [q]
    specs = [lane_block]
    if state is not None:
        operands += list(state)
        specs += [acc_block, ml_block]
    keys_seen = 0
    for source in sources:
        for index, array in enumerate(source):
            if array.ndim == 3:
                specs.append(
                    pl.BlockSpec(
                        (None, array.shape[1], group * HD), lambda g, _, i=index: (i, 0, g)
                    )
                )
            else:
                specs.append(pl.BlockSpec((array.shape[0], group * HD), lambda g, _: (0, g)))
            operands.append(array)
        keys_seen += source[0].shape[-2]
    for _, blocks in stages:
        for bias in blocks:
            if bias is not None:
                operands.append(jnp.asarray(bias))
                specs.append(pl.BlockSpec(bias.shape, lambda g, _: (0, 0)))
    if last:
        out_shape = jax.ShapeDtypeStruct((tokens, width), jnp.bfloat16)
        out_specs = lane_block
        scratch = [
            pltpu.VMEM((group * HD, tokens), jnp.float32),
            pltpu.VMEM((2 * group, tokens), jnp.float32),
        ]
    else:
        out_shape = (
            jax.ShapeDtypeStruct((width, tokens), jnp.float32),
            jax.ShapeDtypeStruct((steps, 2 * group, tokens), jnp.float32),
        )
        out_specs = (acc_block, ml_block)
        scratch = []
    return pl.pallas_call(
        functools.partial(attend_kernel, stages, state is None, last, group),
        out_shape=out_shape,
        grid_spec=pltpu.PrefetchScalarGridSpec(
            num_scalar_prefetch=1,
            grid=(steps,),
            in_specs=specs,
            out_specs=out_specs,
            scratch_shapes=scratch,
        ),
        cost_estimate=pl.CostEstimate(
            flops=4 * tokens * keys_seen * width,
            bytes_accessed=(4 * keys_seen + 8 * tokens) * width,
            transcendentals=tokens * keys_seen * width // HD,
        ),
    )(valid, *operands)


def passed_along(x, axis, by):
    length = lax.axis_size(axis)
    pairs = [(i, i + by) for i in range(length) if 0 <= i + by < length]
    return lax.ppermute(x, axis, pairs)


def gathered(piece, axes):
    held = (piece,)
    for axis in axes:
        distance = lax.axis_size(axis) // 2
        while distance:
            whole = jnp.concatenate(held, axis=1) if len(held) > 1 else held[0]
            pairs = [(i, i ^ distance) for i in range(lax.axis_size(axis))]
            held = (whole, lax.ppermute(whole, axis, pairs))
            distance //= 2
    return held


def local(queries, target_keys, target_values, cond_keys, cond_values):
    view_dev, rows_dev, cols, width = queries.shape
    heads = width // HD
    row_count = lax.axis_size("row")
    view_count = lax.axis_size("view")
    tokens = rows_dev * cols
    row_index = lax.axis_index("row")
    view_index = lax.axis_index("view")
    ctok_dev = cond_keys.shape[0]
    ctok = ctok_dev * view_count * row_count
    group = 4 if heads % 4 == 0 else 1

    partners = jnp.asarray(partner_matrix(), jnp.bfloat16)
    view_table = axis_table(0, view_count * view_dev + 1)
    row_table = axis_table(1, max(row_count * rows_dev, -(-ctok // cols)))
    col_table = axis_table(2, cols)

    cond_ids = np.arange(ctok)
    cond_table = view_table[:, :1] + row_table[:, cond_ids // cols] + col_table[:, cond_ids % cols]
    cond_base = (view_index * row_count + row_index) * ctok_dev
    cond_slice = lax.dynamic_slice_in_dim(jnp.asarray(cond_table), cond_base, ctok_dev, axis=1)
    piece = pl.pallas_call(
        cond_kernel, out_shape=jax.ShapeDtypeStruct((2, ctok_dev, width), jnp.bfloat16)
    )(cond_keys, cond_values, cond_slice, partners)
    cond_held = gathered(piece, ("row", "view"))

    view_dev_ids = view_index * view_dev + 1
    tables = lax.dynamic_slice_in_dim(jnp.asarray(view_table), view_dev_ids, view_dev, axis=1)
    rows_here = lax.dynamic_slice_in_dim(
        jnp.asarray(row_table), row_index * rows_dev, rows_dev, axis=1
    )
    place = (rows_here[:, :, None] + jnp.asarray(col_table)[:, None]).reshape(2, tokens, HD)

    reach = -(-RADIUS // rows_dev)
    near = [d for d in range(1, reach)]
    flags = []
    for d in range(1, reach + 1):
        flags += [row_index - d >= 0, row_index + d < row_count]
    valid = jnp.stack(flags).astype(jnp.int32)

    outputs = []
    for v in range(view_dev):
        values = target_values[v].reshape(tokens, width)
        table = tables[:, v : v + 1] + place
        lane_block = pl.BlockSpec((tokens, 4 * HD), lambda g: (0, g))
        rotate = pl.pallas_call(
            rotate_kernel,
            out_shape=(jax.ShapeDtypeStruct((tokens, width), jnp.bfloat16),) * 2,
            grid=(heads // 4,),
            in_specs=[
                lane_block,
                lane_block,
                pl.BlockSpec((2, tokens, HD), lambda g: (0, 0, 0)),
                pl.BlockSpec((HD, HD), lambda g: (0, 0)),
            ],
            out_specs=(lane_block, lane_block),
            cost_estimate=pl.CostEstimate(
                flops=4 * tokens * width * HD,
                bytes_accessed=8 * tokens * width,
                transcendentals=0,
            ),
            name="rotate",
        )
        q_rot, k_rot = rotate(
            queries[v].reshape(tokens, width),
            target_keys[v].reshape(tokens, width),
            table,
            partners,
        )
        from_above, from_below = [values], [values]
        above, below = [], []
        for _ in range(reach):
            from_above.append(passed_along(from_above[-1], "row", 1))
            from_below.append(passed_along(from_below[-1], "row", -1))
        keys_above, keys_below = k_rot, k_rot
        for d in range(1, reach + 1):
            keys_above = passed_along(keys_above, "row", 1)
            keys_below = passed_along(keys_below, "row", -1)
            above.append((keys_above, from_above[d]))
            below.append((keys_below, from_below[d]))

        def stage_of(d, sign):
            bias = window_bias(rows_dev, cols, sign * d * rows_dev)
            return (2 * (d - 1) + (sign > 0), (bias,))

        state = attend(
            valid, q_rot, None, [(k_rot, values)],
            [(None, (window_bias(rows_dev, cols, 0),))], False, group,
        )
        if near:
            state = attend(
                valid, q_rot, state, [s for d in near for s in (above[d - 1], below[d - 1])],
                [s for d in near for s in (stage_of(d, -1), stage_of(d, 1))], False, group,
            )
        state = attend(
            valid, q_rot, state, [(c, c) for c in cond_held],
            [(None, (None,) * len(cond_held))], False, group,
        )
        out = attend(
            valid, q_rot, state, [above[reach - 1], below[reach - 1]],
            [stage_of(reach, -1), stage_of(reach, 1)], True, group,
        )
        outputs.append(out.reshape(rows_dev, cols, width))
    return jnp.stack(outputs) if view_dev > 1 else outputs[0][None]


def solution(mesh):
    return jax.shard_map(
        local,
        mesh=mesh,
        in_specs=(
            P("view", "row", None, None),
            P("view", "row", None, None),
            P("view", "row", None, None),
            P(("view", "row"), None),
            P(("view", "row"), None),
        ),
        out_specs=P("view", "row", None, None),
        check_vma=False,
    )
```

```python
import functools
from typing import NamedTuple

import jax
import jax.numpy as jnp
import numpy as np
from jax import lax
from jax.experimental import pallas as pl
from jax.experimental.pallas import tpu as pltpu
from jax.sharding import PartitionSpec as P


HD = 128
RADIUS = 8
BASE = 10000.0
NEG = -1e30
KERNEL_VMEM = 16 * 2**20
EXP_SCALE = HD ** (-0.5) * float(np.log2(np.e))


def group_layout(head_dim):
    view_width = head_dim // 4
    row_width = 3 * head_dim // 8
    return (
        (0, view_width),
        (view_width, row_width),
        (view_width + row_width, head_dim - view_width - row_width),
    )


def axis_table(group_index, count):
    offset, width = group_layout(HD)[group_index]
    half = width // 2
    frequency = BASE ** (-np.arange(half, dtype=np.float64) / half)
    angles = np.arange(count, dtype=np.float64)[:, None] * frequency
    cosine = np.zeros((count, HD), np.float32)
    sine = np.zeros((count, HD), np.float32)
    for start in (offset, offset + half):
        cosine[:, start : start + half] = np.cos(angles)
        sine[:, start : start + half] = np.sin(angles)
    return np.stack([cosine, sine])


def partner_matrix():
    m = np.zeros((HD, HD), np.float32)
    for offset, width in group_layout(HD):
        half = width // 2
        for i in range(half):
            m[offset + half + i, offset + i] = -1.0
            m[offset + i, offset + half + i] = 1.0
    return m


def rotated(x, partners, cosine, sine):
    swapped = jnp.dot(x, partners, preferred_element_type=jnp.float32)
    return (x.astype(jnp.float32) * cosine + swapped * sine).astype(jnp.bfloat16)


def cond_kernel(parts, *refs):
    partners_ref, out_ref = refs[3 * parts :]
    for part in range(parts):
        keys_ref, values_ref, table_ref = refs[3 * part : 3 * part + 3]
        count = keys_ref.shape[0]
        here = pl.ds(part * count, count)
        for start in range(0, keys_ref.shape[1], HD):
            span = pl.ds(start, HD)
            out_ref[0, here, span] = rotated(
                keys_ref[:, span], partners_ref[...], table_ref[0], table_ref[1]
            )
        out_ref[1, here] = values_ref[...]


def rotate_kernel(chunks, group, q_ref, k_ref, table_ref, partners_ref, qo_ref, *ko_refs):
    unit = pl.program_id(0)

    def turn(source, start):
        return rotated(
            source[:, pl.ds(start, HD)], partners_ref[...], table_ref[0], table_ref[1]
        )

    for head in range(group):
        qo_ref[:, pl.ds(pl.multiple_of((unit * group + head) * HD, HD), HD)] = turn(
            q_ref, head * HD
        )
    for (first, count), ko_ref in zip(chunks, ko_refs):

        @pl.when((unit * group >= first) & (unit * group < first + count))
        def _(first=first, ko_ref=ko_ref):
            for head in range(group):
                start = pl.multiple_of((unit * group - first + head) * HD, HD)
                ko_ref[:, pl.ds(start, HD)] = turn(k_ref, head * HD)


def mask_tiles(rows, cols, row_shift, lanes):
    tokens = rows * cols
    row = np.arange(tokens) // cols
    col = np.arange(tokens) % cols
    inside = (np.abs(row[:, None] + row_shift - row[None, :]) <= RADIUS) & (
        np.abs(col[:, None] - col[None, :]) <= RADIUS
    )
    tiles, plan = [], []
    for start in range(0, tokens, lanes):
        parts = [inside[r * cols : (r + 1) * cols, start : start + lanes] for r in range(rows)]
        used = [r for r in range(rows) if parts[r].any()]
        names = []
        for r in range(used[0], used[-1] + 1):
            found = [i for i, tile in enumerate(tiles) if (tile == parts[r]).all()]
            if not found:
                tiles.append(parts[r])
            names.append(found[0] if found else len(tiles) - 1)
        plan.append((used[0], used[-1] + 1, tuple(names)))
    return np.where(np.stack(tiles), 0.0, NEG).astype(np.float32), tuple(plan)


def attend_kernel(stages, first, last, group, lanes, *refs):
    refs = list(refs)
    valid_ref, q_ref = refs.pop(0), refs.pop(0)

    def pull(block):
        if block.stacked:
            pair = refs.pop(0)
            return pair.at[0], pair.at[1]
        return refs.pop(0), refs.pop(0)

    pulled = [[pull(b) for b in blocks] for _, blocks in stages]
    masks = [[refs.pop(0) if b.plan else None for b in blocks] for _, blocks in stages]
    if not first:
        acc_in, ml_in = refs.pop(0), refs.pop(0)
    if last is not None:
        if last:
            refs.pop(0)
        out_ref = refs.pop(0)
    acc_ref, ml_ref = refs
    tokens = q_ref.shape[0]
    unit = pl.program_id(0)

    def span_of(head, offset):
        return pl.ds(pl.multiple_of((unit * group + head + offset) * HD, HD), HD)

    def stage(blocks, sources, mask_refs, have):
        def scores(head, start):
            q = q_ref[pl.ds(start, lanes), span_of(head, blocks[0].head)]
            found = []
            for block, (k_ref, _) in zip(blocks, sources):
                low, high = block.rows(start // lanes, k_ref.shape[0])
                k = k_ref[low:high, span_of(head, block.head - block.keys_head)]
                found.append(
                    lax.dot_general(
                        k, q, (((1,), (1,)), ((), ())), preferred_element_type=jnp.float32
                    )
                )
            return found

        def update(head, start, found):
            at = unit * group + head
            here = pl.ds(start, lanes)
            if have:
                top = ml_ref[at, 0:1, here]
                total = ml_ref[at, 1:2, here]
                summed = acc_ref[at, :, here]
            started = have
            for s, block, (k_ref, v_ref), mask_ref in zip(found, blocks, sources, mask_refs):
                low, high = block.rows(start // lanes, k_ref.shape[0])
                if mask_ref is not None:
                    names = block.plan[start // lanes][2]
                    s = s + jnp.concatenate([mask_ref[n] for n in names], axis=0)
                peak = jnp.max(s, axis=0, keepdims=True)
                if started:
                    peak = jnp.maximum(peak, top)
                p = jnp.exp2((s - peak) * EXP_SCALE)
                part = jnp.sum(p, axis=0, keepdims=True)
                v = v_ref[low:high, span_of(head, block.head - block.values_head)]
                pv = lax.dot_general(
                    v, p.astype(jnp.bfloat16), (((0,), (0,)), ((), ())),
                    preferred_element_type=jnp.float32,
                )
                if started:
                    alpha = jnp.exp2((top - peak) * EXP_SCALE)
                    part = part + total * alpha
                    pv = pv + summed * alpha
                top, total, summed, started = peak, part, pv, True
            ml_ref[at, 0:1, here] = top
            ml_ref[at, 1:2, here] = total
            acc_ref[at, :, here] = summed

        work = [(head, start) for head in range(group) for start in range(0, tokens, lanes)]
        ahead = scores(*work[0])
        for index, item in enumerate(work):
            found = ahead
            if index + 1 < len(work):
                ahead = scores(*work[index + 1])
            update(*item, found)

    have = not first
    for (flag, blocks), sources, mask_refs in zip(stages, pulled, masks):
        step = functools.partial(stage, blocks, sources, mask_refs, have)
        if flag is None:
            step()
        else:
            pl.when(valid_ref[flag] != 0)(step)
        have = True
    if last is not None:
        for head in range(group):
            at = unit * group + head
            scaled = acc_ref[at] * (1.0 / ml_ref[at, 1:2, :])
            out_ref[:, pl.ds(head * HD, HD)] = scaled.astype(out_ref.dtype).T


class Block(NamedTuple):
    plan: tuple = ()
    head: int = 0
    keys_head: int = 0
    values_head: int = 0
    cols: int = 0
    stacked: bool = False

    def rows(self, tile, count):
        if not self.plan:
            return 0, count
        return self.plan[tile][0] * self.cols, self.plan[tile][1] * self.cols


def resident(x):
    return pltpu.with_memory_space_constraint(x, pltpu.VMEM)


def attend(valid, q, state, sources, stages, tiles, heads, group, out=None, last=False):
    tokens, width = q.shape
    lanes = 128 if tokens % 128 == 0 else tokens
    first_head = stages[0][1][0].head
    operands = [resident(a) for a in (q, *(a for source in sources for a in source))]
    operands += [resident(jnp.asarray(t)) for t in tiles]
    whole = pl.BlockSpec(memory_space=pltpu.VMEM)
    aliases = {}
    if state is not None:
        aliases = {len(operands) + 1 + i: i + last for i in range(2)}
        operands += [resident(a) for a in state]
    specs = [whole] * len(operands)
    out_shape = [
        pltpu.VMEM((heads, HD, tokens), jnp.float32),
        pltpu.VMEM((heads, 2, tokens), jnp.float32),
    ]
    out_specs = [whole] * 2
    if last:
        out_shape.insert(0, jax.ShapeDtypeStruct((tokens, width), jnp.bfloat16))
        out_specs.insert(
            0, pl.BlockSpec((tokens, group * HD), lambda g, _: (0, first_head // group + g))
        )
        if out is not None:
            aliases[len(operands) + 1] = 0
            operands.append(out)
            specs.append(pl.BlockSpec(memory_space=pl.ANY))
    keys_seen = sum(source[0].shape[-2] for source in sources)
    return pl.pallas_call(
        functools.partial(
            attend_kernel, stages, state is None, (out is not None) if last else None, group, lanes
        ),
        out_shape=out_shape,
        grid_spec=pltpu.PrefetchScalarGridSpec(
            num_scalar_prefetch=1, grid=(heads // group,), in_specs=specs, out_specs=out_specs
        ),
        input_output_aliases=aliases,
        compiler_params=pltpu.CompilerParams(vmem_limit_bytes=KERNEL_VMEM),
        cost_estimate=pl.CostEstimate(
            flops=4 * tokens * keys_seen * heads * HD,
            bytes_accessed=(4 * keys_seen + 8 * tokens) * heads * HD,
            transcendentals=tokens * keys_seen * heads,
        ),
    )(valid, *operands)


def passed_along(x, axis, by):
    length = lax.axis_size(axis)
    pairs = [(i, i + by) for i in range(length) if 0 <= i + by < length]
    return lax.ppermute(x, axis, pairs)


def gathered(piece, steps):
    held = (piece,)
    for axis, distance in steps:
        whole = jnp.concatenate(held, axis=1) if len(held) > 1 else held[0]
        held = (whole, swapped(whole, axis, distance))
    return held


def swapped(x, axis, distance):
    return lax.ppermute(x, axis, [(i, i ^ distance) for i in range(lax.axis_size(axis))])


def swap_steps(mesh_shape):
    steps = []
    for axis in ("row", "view"):
        distance = mesh_shape[axis] // 2
        while distance:
            steps.append((axis, distance))
            distance //= 2
    return steps


def local(queries, target_keys, target_values, cond_keys, cond_values):
    view_dev, rows_dev, cols, width = queries.shape
    heads = width // HD
    row_count = lax.axis_size("row")
    view_count = lax.axis_size("view")
    tokens = rows_dev * cols
    lanes = 128 if tokens % 128 == 0 else tokens
    row_index = lax.axis_index("row")
    view_index = lax.axis_index("view")
    ctok_dev = cond_keys.shape[0]
    ctok = ctok_dev * view_count * row_count
    group = 4 if heads % 4 == 0 else 1
    last_heads = group if heads > group else 0
    chunks = [(0, heads - last_heads)] + [(heads - last_heads, last_heads)] * (last_heads > 0)

    partners = jnp.asarray(partner_matrix(), jnp.bfloat16)
    view_table = axis_table(0, view_count * view_dev + 1)
    row_table = axis_table(1, max(row_count * rows_dev, -(-ctok // cols)))
    col_table = axis_table(2, cols)

    cond_ids = np.arange(ctok)
    cond_table = view_table[:, :1] + row_table[:, cond_ids // cols] + col_table[:, cond_ids % cols]
    steps = swap_steps({"row": row_count, "view": view_count})
    place = {"row": row_index, "view": view_index}

    def cond_part(keys, values, place):
        base = (place["view"] * row_count + place["row"]) * ctok_dev
        table = lax.dynamic_slice_in_dim(jnp.asarray(cond_table), base, ctok_dev, axis=1)
        return keys, values, table

    parts = [cond_part(cond_keys, cond_values, place)]
    if steps:
        axis, distance = steps[0]
        met_keys = swapped(cond_keys, axis, distance)
        met_values = swapped(cond_values, axis, distance)
        met_place = dict(place, **{axis: place[axis] ^ distance})
        parts.append(cond_part(met_keys, met_values, met_place))
    piece = pl.pallas_call(
        functools.partial(cond_kernel, len(parts)),
        out_shape=jax.ShapeDtypeStruct((2, len(parts) * ctok_dev, width), jnp.bfloat16),
        compiler_params=pltpu.CompilerParams(vmem_limit_bytes=KERNEL_VMEM),
        name="join",
    )(*(x for part in parts for x in part), partners)
    cond_held = gathered(piece, steps[1:])

    view_first = view_index * view_dev + 1
    tables = lax.dynamic_slice_in_dim(jnp.asarray(view_table), view_first, view_dev, axis=1)
    rows_here = lax.dynamic_slice_in_dim(
        jnp.asarray(row_table), row_index * rows_dev, rows_dev, axis=1
    )
    in_view = (rows_here[:, :, None] + jnp.asarray(col_table)[:, None]).reshape(2, tokens, HD)

    reach = -(-RADIUS // rows_dev)
    flags = []
    for d in range(1, reach + 1):
        flags += [row_index - d >= 0, row_index + d < row_count]
    valid = jnp.stack(flags).astype(jnp.int32)

    outputs = []
    for v in range(view_dev):
        values = target_values[v].reshape(tokens, width)
        whole = pl.BlockSpec(memory_space=pltpu.VMEM)
        lane_block = pl.BlockSpec((tokens, group * HD), lambda g: (0, g))
        rotate = pl.pallas_call(
            functools.partial(rotate_kernel, chunks, group),
            out_shape=[
                pltpu.VMEM((tokens, width), jnp.bfloat16),
                *(
                    jax.ShapeDtypeStruct((tokens, count * HD), jnp.bfloat16)
                    for _, count in chunks
                ),
            ],
            grid=(heads // group,),
            in_specs=[
                lane_block,
                lane_block,
                pl.BlockSpec((2, tokens, HD), lambda g: (0, 0, 0)),
                pl.BlockSpec((HD, HD), lambda g: (0, 0)),
            ],
            out_specs=[whole] * (1 + len(chunks)),
            compiler_params=pltpu.CompilerParams(vmem_limit_bytes=KERNEL_VMEM),
            cost_estimate=pl.CostEstimate(
                flops=4 * tokens * width * HD, bytes_accessed=8 * tokens * width, transcendentals=0
            ),
            name="rotate",
        )
        q_rot, *k_rot = rotate(
            queries[v].reshape(tokens, width),
            target_keys[v].reshape(tokens, width),
            tables[:, v : v + 1] + in_view,
            partners,
        )

        travels = {"values": values} | {f"keys{c}": k for c, k in enumerate(k_rot)}
        met = {}
        for what, block in travels.items():
            above = below = block
            for d in range(1, reach + 1):
                above = passed_along(above, "row", 1)
                below = passed_along(below, "row", -1)
                met[what, -d], met[what, d] = above, below
            met[what, 0] = block

        out = None
        for c, (first, count) in enumerate(chunks):

            def stage_of(d):
                tiles, plan = mask_tiles(rows_dev, cols, d * rows_dev, lanes)
                block = Block(plan, first, first, 0, cols)
                flag = 2 * (abs(d) - 1) + (d > 0) if d else None
                return (met[f"keys{c}", d], met["values", d]), (flag, (block,)), tiles

            def run(state, picked, **more):
                sources, stages, tiles = zip(*map(stage_of, picked))
                return attend(valid, q_rot, state, sources, stages, tiles, count, group, **more)

            state = run(None, [0])
            near = [d for far in range(1, reach) for d in (-far, far)]
            if near:
                state = run(state, near)
            block = Block((), first, 0, 0, cols, True)
            state = attend(
                valid, q_rot, state, [(x,) for x in cond_held],
                [(None, (block,) * len(cond_held))], [], count, group,
            )
            out, *_ = run(state, [-reach, reach], out=out, last=True)
        outputs.append(out.reshape(rows_dev, cols, width))
    return jnp.stack(outputs) if view_dev > 1 else outputs[0][None]


def solution(mesh):
    return jax.shard_map(
        local,
        mesh=mesh,
        in_specs=(
            P("view", "row", None, None),
            P("view", "row", None, None),
            P("view", "row", None, None),
            P(("view", "row"), None),
            P(("view", "row"), None),
        ),
        out_specs=P("view", "row", None, None),
        check_vma=False,
    )
```

```python
import functools
from typing import NamedTuple

import jax
import jax.numpy as jnp
import numpy as np
from jax import lax
from jax.experimental import pallas as pl
from jax.experimental.pallas import tpu as pltpu
from jax.sharding import PartitionSpec as P


HD = 128
RADIUS = 8
BASE = 10000.0
NEG = -1e30
KERNEL_VMEM = 16 * 2**20
EXP_SCALE = HD ** (-0.5) * float(np.log2(np.e))


def group_layout(head_dim):
    view_width = head_dim // 4
    row_width = 3 * head_dim // 8
    return (
        (0, view_width),
        (view_width, row_width),
        (view_width + row_width, head_dim - view_width - row_width),
    )


def axis_table(group_index, count):
    offset, width = group_layout(HD)[group_index]
    half = width // 2
    frequency = BASE ** (-np.arange(half, dtype=np.float64) / half)
    angles = np.arange(count, dtype=np.float64)[:, None] * frequency
    cosine = np.zeros((count, HD), np.float32)
    sine = np.zeros((count, HD), np.float32)
    for start in (offset, offset + half):
        cosine[:, start : start + half] = np.cos(angles)
        sine[:, start : start + half] = np.sin(angles)
    return np.stack([cosine, sine])


def partner_matrix():
    m = np.zeros((HD, HD), np.float32)
    for offset, width in group_layout(HD):
        half = width // 2
        for i in range(half):
            m[offset + half + i, offset + i] = -1.0
            m[offset + i, offset + half + i] = 1.0
    return m


def rotated(x, partners, cosine, sine):
    swapped = jnp.dot(x, partners, preferred_element_type=jnp.float32)
    return (x.astype(jnp.float32) * cosine + swapped * sine).astype(jnp.bfloat16)


def cond_kernel(parts, *refs):
    partners_ref, out_ref = refs[3 * parts :]
    for part in range(parts):
        keys_ref, values_ref, table_ref = refs[3 * part : 3 * part + 3]
        count = keys_ref.shape[0]
        here = pl.ds(part * count, count)
        for start in range(0, keys_ref.shape[1], HD):
            span = pl.ds(start, HD)
            out_ref[0, here, span] = rotated(
                keys_ref[:, span], partners_ref[...], table_ref[0], table_ref[1]
            )
        out_ref[1, here] = values_ref[...]


def rotate_kernel(chunks, group, q_ref, k_ref, table_ref, partners_ref, qo_ref, *ko_refs):
    unit = pl.program_id(0)

    def turn(source, start):
        return rotated(
            source[:, pl.ds(start, HD)], partners_ref[...], table_ref[0], table_ref[1]
        )

    for head in range(group):
        qo_ref[:, pl.ds(pl.multiple_of((unit * group + head) * HD, HD), HD)] = turn(
            q_ref, head * HD
        )
    for (first, count), ko_ref in zip(chunks, ko_refs):

        @pl.when((unit * group >= first) & (unit * group < first + count))
        def _(first=first, ko_ref=ko_ref):
            for head in range(group):
                start = pl.multiple_of((unit * group - first + head) * HD, HD)
                ko_ref[:, pl.ds(start, HD)] = turn(k_ref, head * HD)


def mask_tiles(rows, cols, row_shift, lanes):
    tokens = rows * cols
    row = np.arange(tokens) // cols
    col = np.arange(tokens) % cols
    inside = (np.abs(row[:, None] + row_shift - row[None, :]) <= RADIUS) & (
        np.abs(col[:, None] - col[None, :]) <= RADIUS
    )
    tiles, plan = [], []
    for start in range(0, tokens, lanes):
        parts = [inside[r * cols : (r + 1) * cols, start : start + lanes] for r in range(rows)]
        used = [r for r in range(rows) if parts[r].any()]
        names = []
        for r in range(used[0], used[-1] + 1):
            found = [i for i, tile in enumerate(tiles) if (tile == parts[r]).all()]
            if not found:
                tiles.append(parts[r])
            names.append(found[0] if found else len(tiles) - 1)
        plan.append((used[0], used[-1] + 1, tuple(names)))
    return np.where(np.stack(tiles), 0.0, NEG).astype(np.float32), tuple(plan)


def attend_kernel(stages, first, last, group, lanes, *refs):
    refs = list(refs)
    q_ref = refs.pop(0)

    def pull(block):
        if block.stacked:
            pair = refs.pop(0)
            return pair.at[0], pair.at[1]
        return refs.pop(0), refs.pop(0)

    pulled = [[pull(b) for b in blocks] for _, blocks in stages]
    masks = [[refs.pop(0) if b.plan else None for b in blocks] for _, blocks in stages]
    if not first:
        acc_in, ml_in = refs.pop(0), refs.pop(0)
    if last is not None:
        if last:
            refs.pop(0)
        out_ref = refs.pop(0)
    acc_ref, ml_ref = refs
    tokens = q_ref.shape[0]
    unit = pl.program_id(0)

    def span_of(head, offset):
        return pl.ds(pl.multiple_of((unit * group + head + offset) * HD, HD), HD)

    def stage(blocks, sources, mask_refs, have):
        def scores(head):
            q = q_ref[:, span_of(head, blocks[0].head)]
            return [
                lax.dot_general(
                    k_ref[:, span_of(head, block.head - block.keys_head)], q,
                    (((1,), (1,)), ((), ())), preferred_element_type=jnp.float32,
                )
                for block, (k_ref, _) in zip(blocks, sources)
            ]

        def update(head, found):
            at = unit * group + head
            if have:
                top, total, summed = ml_ref[at, 0:1], ml_ref[at, 1:2], acc_ref[at]
            started = have
            for s, block, (k_ref, v_ref), mask_ref in zip(found, blocks, sources, mask_refs):
                count = k_ref.shape[0]
                peaks, parts, weights = [], [], []
                for start in range(0, tokens, lanes):
                    here = slice(start, start + lanes)
                    low, high = block.rows(start // lanes, count)
                    seen = s[low:high, here]
                    if mask_ref is not None:
                        names = block.plan[start // lanes][2]
                        seen = seen + jnp.concatenate([mask_ref[n] for n in names], axis=0)
                    peak = jnp.max(seen, axis=0, keepdims=True)
                    if started:
                        peak = jnp.maximum(peak, top[:, here])
                    p = jnp.exp2((seen - peak) * EXP_SCALE)
                    peaks.append(peak)
                    parts.append(jnp.sum(p, axis=0, keepdims=True))
                    p = [p.astype(jnp.bfloat16)]
                    if low:
                        p.insert(0, jnp.zeros((low, lanes), jnp.bfloat16))
                    if high < count:
                        p.append(jnp.zeros((count - high, lanes), jnp.bfloat16))
                    weights.append(jnp.concatenate(p, axis=0) if len(p) > 1 else p[0])
                v = v_ref[:, span_of(head, block.head - block.values_head)]
                pv = lax.dot_general(
                    v, jnp.concatenate(weights, axis=1), (((0,), (0,)), ((), ())),
                    preferred_element_type=jnp.float32,
                )
                peak, part = jnp.concatenate(peaks, axis=1), jnp.concatenate(parts, axis=1)
                if started:
                    alpha = jnp.exp2((top - peak) * EXP_SCALE)
                    part = part + total * alpha
                    pv = pv + summed * alpha
                top, total, summed, started = peak, part, pv, True
            ml_ref[at, 0:1], ml_ref[at, 1:2], acc_ref[at] = top, total, summed

        ahead = scores(0)
        for head in range(group):
            found = ahead
            if head + 1 < group:
                ahead = scores(head + 1)
            update(head, found)


    have = not first
    for (flag, blocks), sources, mask_refs in zip(stages, pulled, masks):
        step = functools.partial(stage, blocks, sources, mask_refs, have)
        if flag is None:
            step()
        else:
            there = lax.axis_index("row") + flag
            pl.when((there >= 0) & (there < lax.axis_size("row")))(step)
        have = True
    if last is not None:
        for head in range(group):
            at = unit * group + head
            scaled = acc_ref[at] * (1.0 / ml_ref[at, 1:2, :])
            out_ref[:, pl.ds(head * HD, HD)] = scaled.astype(out_ref.dtype).T


class Block(NamedTuple):
    plan: tuple = ()
    head: int = 0
    keys_head: int = 0
    values_head: int = 0
    cols: int = 0
    stacked: bool = False

    def rows(self, tile, count):
        if not self.plan:
            return 0, count
        return self.plan[tile][0] * self.cols, self.plan[tile][1] * self.cols


def resident(x):
    return pltpu.with_memory_space_constraint(x, pltpu.VMEM)


def attend(q, state, sources, stages, tiles, heads, group, out=None, last=False):
    tokens, width = q.shape
    lanes = 128 if tokens % 128 == 0 else tokens
    first_head = stages[0][1][0].head
    operands = [resident(a) for a in (q, *(a for source in sources for a in source))]
    operands += [resident(jnp.asarray(t)) for t in tiles]
    whole = pl.BlockSpec(memory_space=pltpu.VMEM)
    aliases = {}
    if state is not None:
        aliases = {len(operands) + i: i + last for i in range(2)}
        operands += [resident(a) for a in state]
    specs = [whole] * len(operands)
    out_shape = [
        pltpu.VMEM((heads, HD, tokens), jnp.float32),
        pltpu.VMEM((heads, 2, tokens), jnp.float32),
    ]
    out_specs = [whole] * 2
    if last:
        out_shape.insert(0, jax.ShapeDtypeStruct((tokens, width), jnp.bfloat16))
        out_specs.insert(
            0, pl.BlockSpec((tokens, group * HD), lambda g: (0, first_head // group + g))
        )
        if out is not None:
            aliases[len(operands)] = 0
            operands.append(out)
            specs.append(pl.BlockSpec(memory_space=pl.ANY))
    keys_seen = sum(source[0].shape[-2] for source in sources)
    return pl.pallas_call(
        functools.partial(
            attend_kernel, stages, state is None, (out is not None) if last else None, group, lanes
        ),
        out_shape=out_shape,
        grid=(heads // group,),
        in_specs=specs,
        out_specs=out_specs,
        input_output_aliases=aliases,
        compiler_params=pltpu.CompilerParams(vmem_limit_bytes=KERNEL_VMEM),
        cost_estimate=pl.CostEstimate(
            flops=4 * tokens * keys_seen * heads * HD,
            bytes_accessed=(4 * keys_seen + 8 * tokens) * heads * HD,
            transcendentals=tokens * keys_seen * heads,
        ),
    )(*operands)


def passed_along(x, axis, by):
    length = lax.axis_size(axis)
    pairs = [(i, i + by) for i in range(length) if 0 <= i + by < length]
    return lax.ppermute(x, axis, pairs)


def gathered(piece, steps):
    held = (piece,)
    for axis, distance in steps:
        whole = jnp.concatenate(held, axis=1) if len(held) > 1 else held[0]
        held = (whole, swapped(whole, axis, distance))
    return held


def swapped(x, axis, distance):
    return lax.ppermute(x, axis, [(i, i ^ distance) for i in range(lax.axis_size(axis))])


def swap_steps(mesh_shape):
    steps = []
    for axis in ("row", "view"):
        distance = mesh_shape[axis] // 2
        while distance:
            steps.append((axis, distance))
            distance //= 2
    return steps


def local(queries, target_keys, target_values, cond_keys, cond_values):
    view_dev, rows_dev, cols, width = queries.shape
    heads = width // HD
    row_count = lax.axis_size("row")
    view_count = lax.axis_size("view")
    tokens = rows_dev * cols
    lanes = 128 if tokens % 128 == 0 else tokens
    row_index = lax.axis_index("row")
    view_index = lax.axis_index("view")
    ctok_dev = cond_keys.shape[0]
    ctok = ctok_dev * view_count * row_count
    group = 4 if heads % 4 == 0 else 1
    last_heads = group if heads > group else 0
    chunks = [(0, heads - last_heads)] + [(heads - last_heads, last_heads)] * (last_heads > 0)

    partners = jnp.asarray(partner_matrix(), jnp.bfloat16)
    view_table = axis_table(0, view_count * view_dev + 1)
    row_table = axis_table(1, max(row_count * rows_dev, -(-ctok // cols)))
    col_table = axis_table(2, cols)

    cond_ids = np.arange(ctok)
    cond_table = view_table[:, :1] + row_table[:, cond_ids // cols] + col_table[:, cond_ids % cols]
    steps = swap_steps({"row": row_count, "view": view_count})
    place = {"row": row_index, "view": view_index}

    def cond_part(keys, values, place):
        base = (place["view"] * row_count + place["row"]) * ctok_dev
        table = lax.dynamic_slice_in_dim(jnp.asarray(cond_table), base, ctok_dev, axis=1)
        return keys, values, table

    parts = [cond_part(cond_keys, cond_values, place)]
    if steps:
        axis, distance = steps[0]
        met_keys = swapped(cond_keys, axis, distance)
        met_values = swapped(cond_values, axis, distance)
        met_place = dict(place, **{axis: place[axis] ^ distance})
        parts.append(cond_part(met_keys, met_values, met_place))
    piece = pl.pallas_call(
        functools.partial(cond_kernel, len(parts)),
        out_shape=jax.ShapeDtypeStruct((2, len(parts) * ctok_dev, width), jnp.bfloat16),
        compiler_params=pltpu.CompilerParams(vmem_limit_bytes=KERNEL_VMEM),
        name="join",
    )(*(x for part in parts for x in part), partners)
    cond_held = gathered(piece, steps[1:])

    view_first = view_index * view_dev + 1
    tables = lax.dynamic_slice_in_dim(jnp.asarray(view_table), view_first, view_dev, axis=1)
    rows_here = lax.dynamic_slice_in_dim(
        jnp.asarray(row_table), row_index * rows_dev, rows_dev, axis=1
    )
    in_view = (rows_here[:, :, None] + jnp.asarray(col_table)[:, None]).reshape(2, tokens, HD)

    reach = -(-RADIUS // rows_dev)
    outputs = []
    for v in range(view_dev):
        values = target_values[v].reshape(tokens, width)
        whole = pl.BlockSpec(memory_space=pltpu.VMEM)
        lane_block = pl.BlockSpec((tokens, group * HD), lambda g: (0, g))
        rotate = pl.pallas_call(
            functools.partial(rotate_kernel, chunks, group),
            out_shape=[
                pltpu.VMEM((tokens, width), jnp.bfloat16),
                *(
                    jax.ShapeDtypeStruct((tokens, count * HD), jnp.bfloat16)
                    for _, count in chunks
                ),
            ],
            grid=(heads // group,),
            in_specs=[
                lane_block,
                lane_block,
                pl.BlockSpec((2, tokens, HD), lambda g: (0, 0, 0)),
                pl.BlockSpec((HD, HD), lambda g: (0, 0)),
            ],
            out_specs=[whole] * (1 + len(chunks)),
            compiler_params=pltpu.CompilerParams(vmem_limit_bytes=KERNEL_VMEM),
            cost_estimate=pl.CostEstimate(
                flops=4 * tokens * width * HD, bytes_accessed=8 * tokens * width, transcendentals=0
            ),
            name="rotate",
        )
        q_rot, *k_rot = rotate(
            queries[v].reshape(tokens, width),
            target_keys[v].reshape(tokens, width),
            tables[:, v : v + 1] + in_view,
            partners,
        )

        travels = {"values": values} | {f"keys{c}": k for c, k in enumerate(k_rot)}
        met = {}
        for what, block in travels.items():
            above = below = block
            for d in range(1, reach + 1):
                above = passed_along(above, "row", 1)
                below = passed_along(below, "row", -1)
                met[what, -d], met[what, d] = above, below
            met[what, 0] = block

        out = None
        for c, (first, count) in enumerate(chunks):

            def stage_of(d):
                tiles, plan = mask_tiles(rows_dev, cols, d * rows_dev, lanes)
                block = Block(plan, first, first, 0, cols)
                return (met[f"keys{c}", d], met["values", d]), (d or None, (block,)), tiles

            def run(state, picked, **more):
                sources, stages, tiles = zip(*map(stage_of, picked))
                return attend(q_rot, state, sources, stages, tiles, count, group, **more)

            state = run(None, [0])
            near = [d for far in range(1, reach) for d in (-far, far)]
            if near:
                state = run(state, near)
            block = Block((), first, 0, 0, cols, True)
            state = attend(
                q_rot, state, [(x,) for x in cond_held],
                [(None, (block,) * len(cond_held))], [], count, group,
            )
            out, *_ = run(state, [-reach, reach], out=out, last=True)
        outputs.append(out.reshape(rows_dev, cols, width))
    return jnp.stack(outputs) if view_dev > 1 else outputs[0][None]


def solution(mesh):
    return jax.shard_map(
        local,
        mesh=mesh,
        in_specs=(
            P("view", "row", None, None),
            P("view", "row", None, None),
            P("view", "row", None, None),
            P(("view", "row"), None),
            P(("view", "row"), None),
        ),
        out_specs=P("view", "row", None, None),
        check_vma=False,
    )
```

```python
import functools
from typing import NamedTuple

import jax
import jax.numpy as jnp
import numpy as np
from jax import lax
from jax.experimental import pallas as pl
from jax.experimental.pallas import tpu as pltpu
from jax.sharding import PartitionSpec as P


HD = 128
RADIUS = 8
BASE = 10000.0
NEG = -1e30
KERNEL_VMEM = 16 * 2**20
EXP_SCALE = HD ** (-0.5) * float(np.log2(np.e))


def group_layout(head_dim):
    view_width = head_dim // 4
    row_width = 3 * head_dim // 8
    return (
        (0, view_width),
        (view_width, row_width),
        (view_width + row_width, head_dim - view_width - row_width),
    )


def axis_table(group_index, count):
    offset, width = group_layout(HD)[group_index]
    half = width // 2
    frequency = BASE ** (-np.arange(half, dtype=np.float64) / half)
    angles = np.arange(count, dtype=np.float64)[:, None] * frequency
    cosine = np.zeros((count, HD), np.float32)
    sine = np.zeros((count, HD), np.float32)
    for start in (offset, offset + half):
        cosine[:, start : start + half] = np.cos(angles)
        sine[:, start : start + half] = np.sin(angles)
    return np.stack([cosine, sine])


def partner_matrix():
    m = np.zeros((HD, HD), np.float32)
    for offset, width in group_layout(HD):
        half = width // 2
        for i in range(half):
            m[offset + half + i, offset + i] = -1.0
            m[offset + i, offset + half + i] = 1.0
    return m


def rotated(x, partners, cosine, sine):
    swapped = jnp.dot(x, partners, preferred_element_type=jnp.float32)
    return (x.astype(jnp.float32) * cosine + swapped * sine).astype(jnp.bfloat16)


def cond_kernel(parts, *refs):
    partners_ref, out_ref = refs[3 * parts :]
    for part in range(parts):
        keys_ref, values_ref, table_ref = refs[3 * part : 3 * part + 3]
        count = keys_ref.shape[0]
        here = pl.ds(part * count, count)
        for start in range(0, keys_ref.shape[1], HD):
            span = pl.ds(start, HD)
            out_ref[0, here, span] = rotated(
                keys_ref[:, span], partners_ref[...], table_ref[0], table_ref[1]
            )
        out_ref[1, here] = values_ref[...]


def rotate_kernel(chunks, q_ref, k_ref, table_ref, partners_ref, qo_ref, lent_ref, *ko_refs):
    def turn(source, head):
        return rotated(
            source[:, pl.ds(head * HD, HD)], partners_ref[...], table_ref[0], table_ref[1]
        )

    for (first, count, _), ko_ref in zip(chunks, ko_refs):
        for head in range(count):
            ko_ref[:, pl.ds(head * HD, HD)] = turn(k_ref, first + head)
    for head in range(q_ref.shape[1] // HD):
        qo_ref[:, pl.ds(head * HD, HD)] = turn(q_ref, head)
    lent_ref[...] = qo_ref[:, pl.ds(chunks[-1][0] * HD, chunks[-1][1] * HD)]


def head_chunks(heads):
    unit = heads // 8
    if heads % 8:
        return ((0, heads, 1),)
    counts, groups = (6 * unit, 2 * unit), (6 * unit, 2 * unit)
    chunks, first = [], 0
    for count, group in zip(counts, groups):
        chunks.append((first, count, group))
        first += count
    return tuple(chunks)


def mask_tiles(rows, cols, row_shift, lanes):
    tokens = rows * cols
    row = np.arange(tokens) // cols
    col = np.arange(tokens) % cols
    inside = (np.abs(row[:, None] + row_shift - row[None, :]) <= RADIUS) & (
        np.abs(col[:, None] - col[None, :]) <= RADIUS
    )
    tiles, plan = [], []
    for start in range(0, tokens, lanes):
        parts = [inside[r * cols : (r + 1) * cols, start : start + lanes] for r in range(rows)]
        used = [r for r in range(rows) if parts[r].any()]
        names = []
        for r in range(used[0], used[-1] + 1):
            found = [i for i, tile in enumerate(tiles) if (tile == parts[r]).all()]
            if not found:
                tiles.append(parts[r])
            names.append(found[0] if found else len(tiles) - 1)
        plan.append((used[0], used[-1] + 1, tuple(names)))
    return np.where(np.stack(tiles), 0.0, NEG).astype(np.float32), tuple(plan)


def attend_kernel(stages, first, last, group, lanes, merge, share, *refs):
    refs = list(refs)
    q_ref = refs.pop(0)

    def pull(block):
        if block.stacked:
            pair = refs.pop(0)
            return pair.at[0], pair.at[1]
        return refs.pop(0), refs.pop(0)

    pulled = [[pull(b) for b in blocks] for _, blocks in stages]
    masks = [[refs.pop(0) if b.plan else None for b in blocks] for _, blocks in stages]
    if not first:
        acc_in, ml_in = refs.pop(0), refs.pop(0)
    if merge is not None:
        part_ref, part_ml_ref = refs.pop(0), refs.pop(0)
    if last is not None:
        if last:
            refs.pop(0)
        out_ref = refs.pop(0)
    if share:
        share_ref, ml_ref, acc_ref = refs
    else:
        acc_ref, ml_ref = refs
    tokens = q_ref.shape[0]
    unit = pl.program_id(0)

    def span_of(head, offset):
        return pl.ds(pl.multiple_of((unit * group + head + offset) * HD, HD), HD)

    def stage(blocks, sources, mask_refs, have):
        def scores(head):
            q = q_ref[:, span_of(head, blocks[0].head)]
            return [
                lax.dot_general(
                    k_ref[:, span_of(head, block.head - block.keys_head)], q,
                    (((1,), (1,)), ((), ())), preferred_element_type=jnp.float32,
                )
                for block, (k_ref, _) in zip(blocks, sources)
            ]

        def update(head, found):
            at = unit * group + head
            if have:
                top, total, summed = ml_ref[at, 0:1], ml_ref[at, 1:2], acc_ref[at]
            started = have
            for s, block, (k_ref, v_ref), mask_ref in zip(found, blocks, sources, mask_refs):
                count = k_ref.shape[0]
                peaks, parts, weights = [], [], []
                for start in range(0, tokens, lanes):
                    here = slice(start, start + lanes)
                    low, high = block.rows(start // lanes, count)
                    seen = s[low:high, here]
                    if mask_ref is not None:
                        names = block.plan[start // lanes][2]
                        seen = seen + jnp.concatenate([mask_ref[n] for n in names], axis=0)
                    peak = jnp.max(seen, axis=0, keepdims=True)
                    if started:
                        peak = jnp.maximum(peak, top[:, here])
                    p = jnp.exp2((seen - peak) * EXP_SCALE)
                    peaks.append(peak)
                    parts.append(jnp.sum(p, axis=0, keepdims=True))
                    p = [p.astype(jnp.bfloat16)]
                    if low:
                        p.insert(0, jnp.zeros((low, lanes), jnp.bfloat16))
                    if high < count:
                        p.append(jnp.zeros((count - high, lanes), jnp.bfloat16))
                    weights.append(jnp.concatenate(p, axis=0) if len(p) > 1 else p[0])
                v = v_ref[:, span_of(head, block.head - block.values_head)]
                pv = lax.dot_general(
                    v, jnp.concatenate(weights, axis=1), (((0,), (0,)), ((), ())),
                    preferred_element_type=jnp.float32,
                )
                peak, part = jnp.concatenate(peaks, axis=1), jnp.concatenate(parts, axis=1)
                if started:
                    alpha = jnp.exp2((top - peak) * EXP_SCALE)
                    part = part + total * alpha
                    pv = pv + summed * alpha
                top, total, summed, started = peak, part, pv, True
            ml_ref[at, 0:1], ml_ref[at, 1:2], acc_ref[at] = top, total, summed

        ahead = scores(0)
        for head in range(group):
            found = ahead
            if head + 1 < group:
                ahead = scores(head + 1)
            update(head, found)


    have = not first
    for (flag, blocks), sources, mask_refs in zip(stages, pulled, masks):
        step = functools.partial(stage, blocks, sources, mask_refs, have)
        if flag is None:
            step()
        else:
            pl.when(flag(lax.axis_index("row"), lax.axis_size("row")))(step)
        have = not share
    if merge is not None:

        @pl.when(merge(lax.axis_index("row"), lax.axis_size("row")))
        def _():
            for head in range(group):
                at = unit * group + head
                top, met = ml_ref[at, 0:1], part_ml_ref[at, 0:1]
                peak = jnp.maximum(top, met)
                ours = jnp.exp2((top - peak) * EXP_SCALE)
                theirs = jnp.exp2((met - peak) * EXP_SCALE) * part_ml_ref[at, 1:2]
                ml_ref[at, 1:2] = ml_ref[at, 1:2] * ours + theirs
                acc_ref[at] = acc_ref[at] * ours + part_ref[at].astype(jnp.float32) * theirs

    if share:
        for head in range(group):
            at = unit * group + head
            share_ref[at] = (acc_ref[at] * (1.0 / ml_ref[at, 1:2])).astype(share_ref.dtype)
    if last is not None:
        for head in range(group):
            at = unit * group + head
            scaled = acc_ref[at] * (1.0 / ml_ref[at, 1:2, :])
            out_ref[:, pl.ds(head * HD, HD)] = scaled.astype(out_ref.dtype).T


class Block(NamedTuple):
    plan: tuple = ()
    head: int = 0
    keys_head: int = 0
    values_head: int = 0
    cols: int = 0
    stacked: bool = False

    def rows(self, tile, count):
        if not self.plan:
            return 0, count
        return self.plan[tile][0] * self.cols, self.plan[tile][1] * self.cols


def resident(x):
    return pltpu.with_memory_space_constraint(x, pltpu.VMEM)


def attend(q, state, sources, stages, tiles, heads, group, out=None, last=False, merge=None, part=(), share=False):
    tokens, width = q.shape
    lanes = 128 if tokens % 128 == 0 else tokens
    first_head = stages[0][1][0].head
    operands = [resident(a) for a in (q, *(a for source in sources for a in source))]
    operands += [resident(jnp.asarray(t)) for t in tiles]
    whole = pl.BlockSpec(memory_space=pltpu.VMEM)
    aliases = {}
    if state is not None:
        aliases = {len(operands) + i: i + last for i in range(2)}
        operands += [resident(a) for a in state]
    operands += [resident(a) for a in part]
    specs = [whole] * len(operands)
    out_shape = [
        pltpu.VMEM((heads, HD, tokens), jnp.float32),
        pltpu.VMEM((heads, 2, tokens), jnp.float32),
    ]
    out_specs = [whole] * 2
    scratch = []
    if share:
        out_shape = [
            jax.ShapeDtypeStruct((heads, HD, tokens), jnp.bfloat16),
            jax.ShapeDtypeStruct((heads, 2, tokens), jnp.float32),
        ]
        scratch = [pltpu.VMEM((heads, HD, tokens), jnp.float32)]
    if last:
        out_shape.insert(0, jax.ShapeDtypeStruct((tokens, width), jnp.bfloat16))
        out_specs.insert(
            0, pl.BlockSpec((tokens, group * HD), lambda g: (0, first_head // group + g))
        )
        if out is not None:
            aliases[len(operands)] = 0
            operands.append(out)
            specs.append(pl.BlockSpec(memory_space=pl.ANY))
    keys_seen = sum(source[0].shape[-2] for source in sources)
    return pl.pallas_call(
        functools.partial(
            attend_kernel, stages, state is None, (out is not None) if last else None, group, lanes,
            merge, share,
        ),
        out_shape=out_shape,
        grid=(heads // group,),
        in_specs=specs,
        out_specs=out_specs,
        scratch_shapes=scratch,
        input_output_aliases=aliases,
        compiler_params=pltpu.CompilerParams(vmem_limit_bytes=KERNEL_VMEM),
        cost_estimate=pl.CostEstimate(
            flops=4 * tokens * keys_seen * heads * HD,
            bytes_accessed=(4 * keys_seen + 8 * tokens) * heads * HD,
            transcendentals=tokens * keys_seen * heads,
        ),
    )(*operands)


def passed_along(x, axis, by, distance, edges=True):
    length = lax.axis_size(axis)
    ends = (-1, length) if edges else (0, length - 1)
    pairs = [
        (i, i + by)
        for i in range(length)
        if ends[0] < i + by < ends[1] and 0 <= i + by - by * distance < length
    ]
    return lax.ppermute(x, axis, pairs)


def gathered(piece, steps):
    held = (piece,)
    for axis, distance in steps:
        whole = jnp.concatenate(held, axis=1) if len(held) > 1 else held[0]
        held = (whole, swapped(whole, axis, distance))
    return held


def swapped(x, axis, distance):
    return lax.ppermute(x, axis, [(i, i ^ distance) for i in range(lax.axis_size(axis))])


def swap_steps(mesh_shape):
    steps = []
    for axis in ("row", "view"):
        distance = mesh_shape[axis] // 2
        while distance:
            steps.append((axis, distance))
            distance //= 2
    return steps


def local(queries, target_keys, target_values, cond_keys, cond_values):
    view_dev, rows_dev, cols, width = queries.shape
    heads = width // HD
    row_count = lax.axis_size("row")
    view_count = lax.axis_size("view")
    tokens = rows_dev * cols
    lanes = 128 if tokens % 128 == 0 else tokens
    row_index = lax.axis_index("row")
    view_index = lax.axis_index("view")
    ctok_dev = cond_keys.shape[0]
    ctok = ctok_dev * view_count * row_count
    chunks = head_chunks(heads)

    partners = jnp.asarray(partner_matrix(), jnp.bfloat16)
    view_table = axis_table(0, view_count * view_dev + 1)
    row_table = axis_table(1, max(row_count * rows_dev, -(-ctok // cols)))
    col_table = axis_table(2, cols)

    cond_ids = np.arange(ctok)
    cond_table = view_table[:, :1] + row_table[:, cond_ids // cols] + col_table[:, cond_ids % cols]
    steps = swap_steps({"row": row_count, "view": view_count})
    place = {"row": row_index, "view": view_index}

    def cond_part(keys, values, place):
        base = (place["view"] * row_count + place["row"]) * ctok_dev
        table = lax.dynamic_slice_in_dim(jnp.asarray(cond_table), base, ctok_dev, axis=1)
        return keys, values, table

    parts = [cond_part(cond_keys, cond_values, place)]
    if steps:
        axis, distance = steps[0]
        met_keys = swapped(cond_keys, axis, distance)
        met_values = swapped(cond_values, axis, distance)
        met_place = dict(place, **{axis: place[axis] ^ distance})
        parts.append(cond_part(met_keys, met_values, met_place))
    piece = pl.pallas_call(
        functools.partial(cond_kernel, len(parts)),
        out_shape=jax.ShapeDtypeStruct((2, len(parts) * ctok_dev, width), jnp.bfloat16),
        compiler_params=pltpu.CompilerParams(vmem_limit_bytes=KERNEL_VMEM),
        name="join",
    )(*(x for part in parts for x in part), partners)
    cond_held = gathered(piece, steps[1:])

    view_first = view_index * view_dev + 1
    tables = lax.dynamic_slice_in_dim(jnp.asarray(view_table), view_first, view_dev, axis=1)
    rows_here = lax.dynamic_slice_in_dim(
        jnp.asarray(row_table), row_index * rows_dev, rows_dev, axis=1
    )
    in_view = (rows_here[:, :, None] + jnp.asarray(col_table)[:, None]).reshape(2, tokens, HD)

    reach = -(-RADIUS // rows_dev)
    outputs = []
    for v in range(view_dev):
        values = target_values[v].reshape(tokens, width)
        whole = pl.BlockSpec(memory_space=pltpu.VMEM)
        rotate = pl.pallas_call(
            functools.partial(rotate_kernel, chunks),
            out_shape=[
                pltpu.VMEM((tokens, width), jnp.bfloat16),
                jax.ShapeDtypeStruct((tokens, chunks[-1][1] * HD), jnp.bfloat16),
                *(
                    jax.ShapeDtypeStruct((tokens, count * HD), jnp.bfloat16)
                    for _, count, _ in chunks
                ),
            ],
            in_specs=[whole] * 4,
            out_specs=[whole] * (2 + len(chunks)),
            compiler_params=pltpu.CompilerParams(vmem_limit_bytes=KERNEL_VMEM),
            cost_estimate=pl.CostEstimate(
                flops=4 * tokens * width * HD, bytes_accessed=8 * tokens * width, transcendentals=0
            ),
            name="rotate",
        )
        q_rot, q_lent, *k_rot = rotate(
            resident(queries[v].reshape(tokens, width)),
            resident(target_keys[v].reshape(tokens, width)),
            resident(tables[:, v : v + 1] + in_view),
            resident(partners),
        )

        lend = row_count >= 4 and reach == 2 and len(chunks) > 1
        lent = len(chunks) - 1
        met = {}

        def travel(what, block, near_only=False):
            met[what, 0] = block
            above = below = block
            for d in range(1, 2 if near_only else reach + 1):
                edges = not (lend and d == reach and what in (f"keys{lent}", f"values{lent}"))
                above = passed_along(above, "row", 1, d, edges)
                below = passed_along(below, "row", -1, d, edges)
                met[what, -d], met[what, d] = above, below

        for c, keys in enumerate(k_rot):
            travel(f"keys{c}", keys)
        if lend:
            travel("values", values, near_only=True)
            for c, (first, count, _) in enumerate(chunks):
                span = slice(first * HD, (first + count) * HD)
                for sign, by in ((-1, 1), (1, -1)):
                    edges = c != lent
                    met[f"values{c}", 2 * sign] = passed_along(
                        met["values", sign][:, span], "row", by, 2, edges
                    )
        else:
            travel("values", values)

        def block_of(c, d, shift=None):
            first = chunks[c][0]
            tiles, plan = mask_tiles(rows_dev, cols, (d if shift is None else shift) * rows_dev, lanes)
            split = (f"values{c}", d) in met
            pair = met[f"keys{c}", d], met[f"values{c}" if split else "values", d]
            return pair, Block(plan, first, first, first if split else 0, cols), tiles

        def within(d):
            return lambda index, size: (index + d >= 0) & (index + d < size)

        part = ()
        if lend:
            first, count, group = chunks[lent]
            last_row = row_count - 1
            asked = lax.ppermute(q_lent, "row", [(0, 1), (last_row, last_row - 1)])
            pairs, blocks, tiles = zip(block_of(lent, 1, 2), block_of(lent, -1, -2))
            blocks = [b._replace(head=0, keys_head=0, values_head=-first) for b in blocks]
            stages = [
                (lambda index, size: index == 1, (blocks[0],)),
                (lambda index, size: index == size - 2, (blocks[1],)),
            ]
            quotients, totals = attend(asked, None, pairs, stages, tiles, count, group, share=True)
            back = [(1, 0), (last_row - 1, last_row)]
            part = (lax.ppermute(quotients, "row", back),)
            part += (lax.ppermute(totals, "row", back),)

        out = None
        for c, (first, count, group) in enumerate(chunks):

            def run(state, picked, flags, **more):
                pairs, blocks, tiles = zip(*(block_of(c, d) for d in picked))
                stages = [(flag, (block,)) for flag, block in zip(flags, blocks)]
                return attend(q_rot, state, pairs, stages, tiles, count, group, **more)

            state = run(None, [0], [None])
            near = [d for far in range(1, reach) for d in (-far, far)]
            if near:
                state = run(state, near, [within(d) for d in near])
            block = Block((), first, 0, 0, cols, True)
            state = attend(
                q_rot, state, [(x,) for x in cond_held],
                [(None, (block,) * len(cond_held))], [], count, group,
            )
            flags, more = [within(-reach), within(reach)], {}
            if lend and c == lent:
                flags = [
                    lambda index, size: (index >= reach) & (index < size - 1),
                    lambda index, size: (index > 0) & (index < size - reach),
                ]
                more = dict(
                    merge=lambda index, size: (index == 0) | (index == size - 1), part=part
                )
            out, *_ = run(state, [-reach, reach], flags, out=out, last=True, **more)
        outputs.append(out.reshape(rows_dev, cols, width))
    return jnp.stack(outputs) if view_dev > 1 else outputs[0][None]


def solution(mesh):
    return jax.shard_map(
        local,
        mesh=mesh,
        in_specs=(
            P("view", "row", None, None),
            P("view", "row", None, None),
            P("view", "row", None, None),
            P(("view", "row"), None),
            P(("view", "row"), None),
        ),
        out_specs=P("view", "row", None, None),
        check_vma=False,
    )
```

```python
import functools
from typing import NamedTuple

import jax
import jax.numpy as jnp
import numpy as np
from jax import lax
from jax.experimental import pallas as pl
from jax.experimental.pallas import tpu as pltpu
from jax.sharding import PartitionSpec as P


HD = 128
RADIUS = 8
BASE = 10000.0
NEG = -1e30
KERNEL_VMEM = 16 * 2**20
EXP_SCALE = HD ** (-0.5) * float(np.log2(np.e))


def group_layout(head_dim):
    view_width = head_dim // 4
    row_width = 3 * head_dim // 8
    return (
        (0, view_width),
        (view_width, row_width),
        (view_width + row_width, head_dim - view_width - row_width),
    )


def axis_table(group_index, count):
    offset, width = group_layout(HD)[group_index]
    half = width // 2
    frequency = BASE ** (-np.arange(half, dtype=np.float64) / half)
    angles = np.arange(count, dtype=np.float64)[:, None] * frequency
    cosine = np.zeros((count, HD), np.float32)
    sine = np.zeros((count, HD), np.float32)
    for start in (offset, offset + half):
        cosine[:, start : start + half] = np.cos(angles)
        sine[:, start : start + half] = np.sin(angles)
    return np.stack([cosine, sine])


def partner_matrix():
    m = np.zeros((HD, HD), np.float32)
    for offset, width in group_layout(HD):
        half = width // 2
        for i in range(half):
            m[offset + half + i, offset + i] = -1.0
            m[offset + i, offset + half + i] = 1.0
    return m


def rotated(x, partners, cosine, sine):
    swapped = jnp.dot(x, partners, preferred_element_type=jnp.float32)
    return (x.astype(jnp.float32) * cosine + swapped * sine).astype(jnp.bfloat16)


def cond_kernel(parts, *refs):
    partners_ref, out_ref = refs[3 * parts :]
    for part in range(parts):
        keys_ref, values_ref, table_ref = refs[3 * part : 3 * part + 3]
        count = keys_ref.shape[0]
        here = pl.ds(part * count, count)
        for start in range(0, keys_ref.shape[1], HD):
            span = pl.ds(start, HD)
            out_ref[0, here, span] = rotated(
                keys_ref[:, span], partners_ref[...], table_ref[0], table_ref[1]
            )
        out_ref[1, here] = values_ref[...]


def rotate_kernel(chunks, q_ref, k_ref, table_ref, partners_ref, qo_ref, lent_ref, *ko_refs):
    def turn(source, head):
        return rotated(
            source[:, pl.ds(head * HD, HD)], partners_ref[...], table_ref[0], table_ref[1]
        )

    for (first, count, _), ko_ref in zip(chunks, ko_refs):
        for head in range(count):
            ko_ref[:, pl.ds(head * HD, HD)] = turn(k_ref, first + head)
    for head in range(q_ref.shape[1] // HD):
        qo_ref[:, pl.ds(head * HD, HD)] = turn(q_ref, head)
    lent_ref[...] = qo_ref[:, pl.ds(chunks[-1][0] * HD, chunks[-1][1] * HD)]


def head_chunks(heads):
    unit = heads // 8
    if heads % 8:
        return ((0, heads, 1),)
    counts, groups = (4 * unit, 4 * unit), (4 * unit, 2 * unit)
    chunks, first = [], 0
    for count, group in zip(counts, groups):
        chunks.append((first, count, group))
        first += count
    return tuple(chunks)


def mask_tiles(rows, cols, row_shift, lanes):
    tokens = rows * cols
    row = np.arange(tokens) // cols
    col = np.arange(tokens) % cols
    inside = (np.abs(row[:, None] + row_shift - row[None, :]) <= RADIUS) & (
        np.abs(col[:, None] - col[None, :]) <= RADIUS
    )
    tiles, plan = [], []
    for start in range(0, tokens, lanes):
        parts = [inside[r * cols : (r + 1) * cols, start : start + lanes] for r in range(rows)]
        used = [r for r in range(rows) if parts[r].any()] or [0]
        names = []
        for r in range(used[0], used[-1] + 1):
            found = [i for i, tile in enumerate(tiles) if (tile == parts[r]).all()]
            if not found:
                tiles.append(parts[r])
            names.append(found[0] if found else len(tiles) - 1)
        plan.append((used[0], used[-1] + 1, tuple(names)))
    return np.where(np.stack(tiles), 0.0, NEG).astype(np.float32), tuple(plan)


def attend_kernel(stages, first, last, group, lanes, merge, share, base, *refs):
    refs = list(refs)
    q_ref = refs.pop(0)

    def pull(block):
        if block.stacked:
            pair = refs.pop(0)
            return pair.at[0], pair.at[1]
        return refs.pop(0), refs.pop(0)

    pulled = [[pull(b) for b in blocks] for _, blocks in stages]
    masks = [[refs.pop(0) if b.plan else None for b in blocks] for _, blocks in stages]
    if not first:
        acc_in, ml_in = refs.pop(0), refs.pop(0)
    if merge is not None:
        part_ref, part_ml_ref = refs.pop(0), refs.pop(0)
    if last is not None:
        if last:
            refs.pop(0)
        out_ref = refs.pop(0)
    if share:
        share_ref, ml_ref, acc_ref = refs
    else:
        acc_ref, ml_ref = refs
    tokens = q_ref.shape[0]
    unit = pl.program_id(0)

    def span_of(head, offset):
        return pl.ds(pl.multiple_of((unit * group + head + offset) * HD, HD), HD)

    def stage(blocks, sources, mask_refs, have):
        def scores(head):
            q = q_ref[:, span_of(head, blocks[0].head)]
            return [
                lax.dot_general(
                    k_ref[:, span_of(head, block.head - block.keys_head)], q,
                    (((1,), (1,)), ((), ())), preferred_element_type=jnp.float32,
                )
                for block, (k_ref, _) in zip(blocks, sources)
            ]

        def update(head, found):
            at = base + unit * group + head
            if have:
                top, total, summed = ml_ref[at, 0:1], ml_ref[at, 1:2], acc_ref[at]
            started = have
            for s, block, (k_ref, v_ref), mask_ref in zip(found, blocks, sources, mask_refs):
                count = k_ref.shape[0]
                peaks, parts, weights = [], [], []
                for start in range(0, tokens, lanes):
                    here = slice(start, start + lanes)
                    low, high = block.rows(start // lanes, count)
                    seen = s[low:high, here]
                    if mask_ref is not None:
                        names = block.plan[start // lanes][2]
                        seen = seen + jnp.concatenate([mask_ref[n] for n in names], axis=0)
                    peak = jnp.max(seen, axis=0, keepdims=True)
                    if started:
                        peak = jnp.maximum(peak, top[:, here])
                    p = jnp.exp2((seen - peak) * EXP_SCALE)
                    peaks.append(peak)
                    parts.append(jnp.sum(p, axis=0, keepdims=True))
                    p = [p.astype(jnp.bfloat16)]
                    if low:
                        p.insert(0, jnp.zeros((low, lanes), jnp.bfloat16))
                    if high < count:
                        p.append(jnp.zeros((count - high, lanes), jnp.bfloat16))
                    weights.append(jnp.concatenate(p, axis=0) if len(p) > 1 else p[0])
                v = v_ref[:, span_of(head, block.head - block.values_head)]
                pv = lax.dot_general(
                    v, jnp.concatenate(weights, axis=1), (((0,), (0,)), ((), ())),
                    preferred_element_type=jnp.float32,
                )
                peak, part = jnp.concatenate(peaks, axis=1), jnp.concatenate(parts, axis=1)
                if started:
                    alpha = jnp.exp2((top - peak) * EXP_SCALE)
                    part = part + total * alpha
                    pv = pv + summed * alpha
                top, total, summed, started = peak, part, pv, True
            ml_ref[at, 0:1], ml_ref[at, 1:2], acc_ref[at] = top, total, summed

        ahead = scores(0)
        for head in range(group):
            found = ahead
            if head + 1 < group:
                ahead = scores(head + 1)
            update(head, found)


    have = not first
    for (flag, blocks), sources, mask_refs in zip(stages, pulled, masks):
        step = functools.partial(stage, blocks, sources, mask_refs, have)
        if flag is None:
            step()
        else:
            pl.when(flag(lax.axis_index("row"), lax.axis_size("row")))(step)
        have = not share
    if merge is not None:

        @pl.when(merge(lax.axis_index("row"), lax.axis_size("row")))
        def _():
            for head in range(group):
                at = base + unit * group + head
                top, met = ml_ref[at, 0:1], part_ml_ref[at, 0:1]
                peak = jnp.maximum(top, met)
                ours = jnp.exp2((top - peak) * EXP_SCALE)
                theirs = jnp.exp2((met - peak) * EXP_SCALE) * part_ml_ref[at, 1:2]
                ml_ref[at, 1:2] = ml_ref[at, 1:2] * ours + theirs
                acc_ref[at] = acc_ref[at] * ours + part_ref[at].astype(jnp.float32) * theirs

    if share:
        for head in range(group):
            at = base + unit * group + head
            share_ref[at] = (acc_ref[at] * (1.0 / ml_ref[at, 1:2])).astype(share_ref.dtype)
    if last is not None:
        for head in range(group):
            at = base + unit * group + head
            scaled = acc_ref[at] * (1.0 / ml_ref[at, 1:2, :])
            out_ref[:, pl.ds(head * HD, HD)] = scaled.astype(out_ref.dtype).T


class Block(NamedTuple):
    plan: tuple = ()
    head: int = 0
    keys_head: int = 0
    values_head: int = 0
    cols: int = 0
    stacked: bool = False

    def rows(self, tile, count):
        if not self.plan:
            return 0, count
        return self.plan[tile][0] * self.cols, self.plan[tile][1] * self.cols


def resident(x):
    return pltpu.with_memory_space_constraint(x, pltpu.VMEM)


def attend(
    q, state, sources, stages, tiles, heads, group, out=None, last=False, merge=None, part=(), share=False,
    base=0,
):
    tokens, width = q.shape
    lanes = 128 if tokens % 128 == 0 else tokens
    first_head = stages[0][1][0].head
    operands = [resident(a) for a in (q, *(a for source in sources for a in source))]
    operands += [resident(jnp.asarray(t)) for t in tiles]
    whole = pl.BlockSpec(memory_space=pltpu.VMEM)
    aliases = {}
    if state is not None:
        aliases = {len(operands) + i: i + last for i in range(2)}
        operands += [resident(a) for a in state]
    operands += [resident(a) for a in part]
    specs = [whole] * len(operands)
    held = heads if state is None else state[0].shape[0]
    out_shape = [
        pltpu.VMEM((held, HD, tokens), jnp.float32),
        pltpu.VMEM((held, 2, tokens), jnp.float32),
    ]
    out_specs = [whole] * 2
    scratch = []
    if share:
        out_shape = [
            jax.ShapeDtypeStruct((heads, HD, tokens), jnp.bfloat16),
            jax.ShapeDtypeStruct((heads, 2, tokens), jnp.float32),
        ]
        scratch = [pltpu.VMEM((heads, HD, tokens), jnp.float32)]
    if last:
        out_shape.insert(0, jax.ShapeDtypeStruct((tokens, width), jnp.bfloat16))
        out_specs.insert(
            0, pl.BlockSpec((tokens, group * HD), lambda g: (0, first_head // group + g))
        )
        if out is not None:
            aliases[len(operands)] = 0
            operands.append(out)
            specs.append(pl.BlockSpec(memory_space=pl.ANY))
    keys_seen = sum(source[0].shape[-2] for source in sources)
    return pl.pallas_call(
        functools.partial(
            attend_kernel, stages, state is None, (out is not None) if last else None, group, lanes,
            merge, share, base,
        ),
        out_shape=out_shape,
        grid=(heads // group,),
        in_specs=specs,
        out_specs=out_specs,
        scratch_shapes=scratch,
        input_output_aliases=aliases,
        compiler_params=pltpu.CompilerParams(vmem_limit_bytes=KERNEL_VMEM),
        cost_estimate=pl.CostEstimate(
            flops=4 * tokens * keys_seen * heads * HD,
            bytes_accessed=(4 * keys_seen + 8 * tokens) * heads * HD,
            transcendentals=tokens * keys_seen * heads,
        ),
    )(*operands)


def passed_along(x, axis, by, distance, edges=True):
    length = lax.axis_size(axis)
    ends = (-1, length) if edges else (0, length - 1)
    pairs = [
        (i, i + by)
        for i in range(length)
        if ends[0] < i + by < ends[1] and 0 <= i + by - by * distance < length
    ]
    return lax.ppermute(x, axis, pairs)


def gathered(piece, steps):
    held = (piece,)
    for axis, distance in steps:
        whole = jnp.concatenate(held, axis=1) if len(held) > 1 else held[0]
        held = (whole, swapped(whole, axis, distance))
    return held


def swapped(x, axis, distance):
    return lax.ppermute(x, axis, [(i, i ^ distance) for i in range(lax.axis_size(axis))])


def swap_steps(mesh_shape):
    steps = []
    for axis in ("row", "view"):
        distance = mesh_shape[axis] // 2
        while distance:
            steps.append((axis, distance))
            distance //= 2
    return steps


def local(queries, target_keys, target_values, cond_keys, cond_values):
    view_dev, rows_dev, cols, width = queries.shape
    heads = width // HD
    row_count = lax.axis_size("row")
    view_count = lax.axis_size("view")
    tokens = rows_dev * cols
    lanes = 128 if tokens % 128 == 0 else tokens
    row_index = lax.axis_index("row")
    view_index = lax.axis_index("view")
    ctok_dev = cond_keys.shape[0]
    ctok = ctok_dev * view_count * row_count
    chunks = head_chunks(heads)

    partners = jnp.asarray(partner_matrix(), jnp.bfloat16)
    view_table = axis_table(0, view_count * view_dev + 1)
    row_table = axis_table(1, max(row_count * rows_dev, -(-ctok // cols)))
    col_table = axis_table(2, cols)

    cond_ids = np.arange(ctok)
    cond_table = view_table[:, :1] + row_table[:, cond_ids // cols] + col_table[:, cond_ids % cols]
    steps = swap_steps({"row": row_count, "view": view_count})
    place = {"row": row_index, "view": view_index}

    def cond_part(keys, values, place):
        base = (place["view"] * row_count + place["row"]) * ctok_dev
        table = lax.dynamic_slice_in_dim(jnp.asarray(cond_table), base, ctok_dev, axis=1)
        return keys, values, table

    parts = [cond_part(cond_keys, cond_values, place)]
    if steps:
        axis, distance = steps[0]
        met_keys = swapped(cond_keys, axis, distance)
        met_values = swapped(cond_values, axis, distance)
        met_place = dict(place, **{axis: place[axis] ^ distance})
        parts.append(cond_part(met_keys, met_values, met_place))
    piece = pl.pallas_call(
        functools.partial(cond_kernel, len(parts)),
        out_shape=jax.ShapeDtypeStruct((2, len(parts) * ctok_dev, width), jnp.bfloat16),
        compiler_params=pltpu.CompilerParams(vmem_limit_bytes=KERNEL_VMEM),
        name="join",
    )(*(x for part in parts for x in part), partners)
    cond_held = gathered(piece, steps[1:])

    view_first = view_index * view_dev + 1
    tables = lax.dynamic_slice_in_dim(jnp.asarray(view_table), view_first, view_dev, axis=1)
    rows_here = lax.dynamic_slice_in_dim(
        jnp.asarray(row_table), row_index * rows_dev, rows_dev, axis=1
    )
    in_view = (rows_here[:, :, None] + jnp.asarray(col_table)[:, None]).reshape(2, tokens, HD)

    reach = -(-RADIUS // rows_dev)
    outputs = []
    for v in range(view_dev):
        values = target_values[v].reshape(tokens, width)
        whole = pl.BlockSpec(memory_space=pltpu.VMEM)
        rotate = pl.pallas_call(
            functools.partial(rotate_kernel, chunks),
            out_shape=[
                pltpu.VMEM((tokens, width), jnp.bfloat16),
                jax.ShapeDtypeStruct((tokens, chunks[-1][1] * HD), jnp.bfloat16),
                *(
                    jax.ShapeDtypeStruct((tokens, count * HD), jnp.bfloat16)
                    for _, count, _ in chunks
                ),
            ],
            in_specs=[whole] * 4,
            out_specs=[whole] * (2 + len(chunks)),
            compiler_params=pltpu.CompilerParams(vmem_limit_bytes=KERNEL_VMEM),
            cost_estimate=pl.CostEstimate(
                flops=4 * tokens * width * HD, bytes_accessed=8 * tokens * width, transcendentals=0
            ),
            name="rotate",
        )
        q_rot, q_lent, *k_rot = rotate(
            resident(queries[v].reshape(tokens, width)),
            resident(target_keys[v].reshape(tokens, width)),
            resident(tables[:, v : v + 1] + in_view),
            resident(partners),
        )

        lend = row_count >= 4 and reach == 2 and len(chunks) > 1
        lent = len(chunks) - 1
        met = {}

        def travel(what, block, near_only=False):
            met[what, 0] = block
            above = below = block
            for d in range(1, 2 if near_only else reach + 1):
                above = passed_along(above, "row", 1, d)
                below = passed_along(below, "row", -1, d)
                met[what, -d], met[what, d] = above, below

        for c, keys in enumerate(k_rot):
            travel(f"keys{c}", keys, near_only=lend and c == lent)
        if lend:
            travel("values", values, near_only=True)
            for c, (first, count, _) in enumerate(chunks):
                span = slice(first * HD, (first + count) * HD)
                for sign, by in ((-1, 1), (1, -1)):
                    edges = c != lent
                    met[f"values{c}", 2 * sign] = passed_along(
                        met["values", sign][:, span], "row", by, 2, edges
                    )
            halves = [(half * chunks[lent][2], chunks[lent][2]) for half in range(chunks[lent][1] // chunks[lent][2])]
            for half, (offset, count) in enumerate(halves):
                span = slice(offset * HD, (offset + count) * HD)
                for sign, by in ((-1, 1), (1, -1)):
                    met[f"half{half}", 2 * sign] = passed_along(met[f"keys{lent}", sign][:, span], "row", by, 2, False)
        else:
            travel("values", values)

        def block_of(c, d, shift=None, half=None):
            first = chunks[c][0]
            tiles, plan = mask_tiles(rows_dev, cols, (d if shift is None else shift) * rows_dev, lanes)
            split = (f"values{c}", d) in met
            held = met[f"values{c}" if split else "values", d]
            values_head = first if split else 0
            if half is not None:
                head = first + halves[half][0]
                return (met[f"half{half}", d], held), Block(plan, head, head, values_head, cols), tiles
            return (met[f"keys{c}", d], held), Block(plan, first, first, values_head, cols), tiles

        def within(d):
            return lambda index, size: (index + d >= 0) & (index + d < size)

        part = ()
        if lend:
            first, count, group = chunks[lent]
            last_row = row_count - 1
            asked = lax.ppermute(q_lent, "row", [(0, 1), (last_row, last_row - 1)])
            pairs, blocks, tiles = zip(block_of(lent, 1, 2), block_of(lent, -1, -2))
            blocks = [b._replace(head=0, keys_head=0, values_head=-first) for b in blocks]
            stages = [
                (lambda index, size: index == 1, (blocks[0],)),
                (lambda index, size: index == size - 2, (blocks[1],)),
            ]
            quotients, totals = attend(asked, None, pairs, stages, tiles, count, group, share=True)
            back = [(1, 0), (last_row - 1, last_row)]
            part = (lax.ppermute(quotients, "row", back),)
            part += (lax.ppermute(totals, "row", back),)

        out = None
        for c, (first, count, group) in enumerate(chunks):

            def run(state, picked, flags, **more):
                pairs, blocks, tiles = zip(*(block_of(c, d) for d in picked))
                stages = [(flag, (block,)) for flag, block in zip(flags, blocks)]
                return attend(q_rot, state, pairs, stages, tiles, count, group, **more)

            state = run(None, [0], [None])
            near = [d for far in range(1, reach) for d in (-far, far)]
            if near:
                state = run(state, near, [within(d) for d in near])
            block = Block((), first, 0, 0, cols, True)
            state = attend(
                q_rot, state, [(x,) for x in cond_held],
                [(None, (block,) * len(cond_held))], [], count, group,
            )
            if not (lend and c == lent):
                out, *_ = run(state, [-reach, reach], [within(-reach), within(reach)], out=out, last=True)
                continue
            flags = [
                lambda index, size: (index >= reach) & (index < size - 1),
                lambda index, size: (index > 0) & (index < size - reach),
            ]
            for half, (offset, count) in enumerate(halves):
                pairs, blocks, tiles = zip(*(block_of(c, d, None, half) for d in (-reach, reach)))
                stages = [(flag, (block,)) for flag, block in zip(flags, blocks)]
                out, *state = attend(
                    q_rot, state, pairs, stages, tiles, count, group, out=out,
                    last=True, base=offset, part=part,
                    merge=lambda index, size: (index == 0) | (index == size - 1),
                )
        outputs.append(out.reshape(rows_dev, cols, width))
    return jnp.stack(outputs) if view_dev > 1 else outputs[0][None]


def solution(mesh):
    return jax.shard_map(
        local,
        mesh=mesh,
        in_specs=(
            P("view", "row", None, None),
            P("view", "row", None, None),
            P("view", "row", None, None),
            P(("view", "row"), None),
            P(("view", "row"), None),
        ),
        out_specs=P("view", "row", None, None),
        check_vma=False,
    )
```
